256 devices in a mesh: view: 16 (over y_lo, x, core), bulk: 16 (over y_hi, z).
Axes of the slice: x: 4, y: 4 (y_hi: 2, y_lo: 2; y = y_hi * 2 + y_lo), z: 8, core: 2. Of those that a mesh axis runs over, the one named last changes fastest.
Arguments:
- estimate: float32 [512, 32, 512], P('bulk'), may hold values from 0.5 to 2
- image: float32 [16, 512, 32, 512], P('view', 'bulk'), may hold values from 0.05 to 20, as said below
- psf: float32 [16, 3, 15], P('view'), may hold values from 0.05 to 1
- perm: int32 [16], P('view'), may hold values from 0 to 1
- shift: int32 [16], P('view'), may hold values from -8 to 7
- visible: int32 [16, 512], P('view', 'bulk'), may hold values 0 or 1
Outputs:
- updated: float32 [512, 32, 512], P('bulk')
The draws below stay inside these ranges and needn't reach their ends.
Inputs may be any that keep to these rules, and one draw needn't show every extreme that they name: `image`: every entry is positive.
All inputs are finite; a program needn't handle non-finite values. No bound on the sum of `visible` on one device may be relied on, other than what follows from the above.
Results may differ from the reference program's by a relative error of at most 0.0003.
Values sent between devices are 32-bit elements; how exact they have to be, the bound alone decides.
A program may use at most 128 MiB of HBM per device.

```python
import math
import jax
import jax.numpy as jnp
from jax import lax

NY = 32
TAPS = 15
VIEWS = 16
NZ = 512
NX = 512


def draw_image(key, part):
    rough_key, size_key, sign_key, phase_key = jax.random.split(key, 4)
    shape = (VIEWS, NZ, NY, NX)
    rough = jnp.exp(jax.random.uniform(rough_key, shape, jnp.float32, math.log(0.5), math.log(2.0)))
    amplitude = 0.45
    magnitude = jax.random.uniform(size_key, (VIEWS, 4, 3), jnp.float32, 1.0 / 64.0, 1.0 / 24.0)
    signs = jnp.where(jax.random.bernoulli(sign_key, 0.5, (VIEWS, 4, 3)), 1.0, -1.0).astype(jnp.float32)
    freqs = magnitude * signs
    phases = jax.random.uniform(phase_key, (VIEWS, 4), jnp.float32, 0.0, 1.0)
    zpos = jnp.arange(NZ, dtype=jnp.float32)[None, :, None, None]
    ypos = jnp.arange(NY, dtype=jnp.float32)[None, None, :, None]
    xpos = jnp.arange(NX, dtype=jnp.float32)[None, None, None, :]
    field = jnp.zeros(shape, jnp.float32)
    for wave in range(4):
        along_z = jnp.mod(freqs[:, wave, 0][:, None, None, None] * zpos, 1.0)
        along_y = jnp.mod(freqs[:, wave, 1][:, None, None, None] * ypos, 1.0)
        along_x = jnp.mod(freqs[:, wave, 2][:, None, None, None] * xpos, 1.0)
        cycles = jnp.mod(along_z + along_y + along_x + phases[:, wave][:, None, None, None], 1.0)
        field = field + jnp.cos(2.0 * math.pi * cycles)
    return (rough * jnp.exp(amplitude * field)).astype(jnp.float32)


def with_ends(entries, own_key, low, high):
    longest = entries.shape.index(max(entries.shape))
    spots = []
    for shift in (0, 1):
        where = [jax.random.randint(jax.random.fold_in(own_key, axis), (), 0, length) for axis, length in enumerate(entries.shape)]
        where[longest] = (where[longest] + shift) % entries.shape[longest]
        spots.append(tuple(where))
    return entries.at[spots[0]].set(low).at[spots[1]].set(high)


def block_levels(key, dims, cuts, smallest, top_value):
    def one(dim, shards_of):
        steps = jax.random.uniform(jax.random.fold_in(jax.random.fold_in(key, 6), dim), (shards_of,), jnp.float32, smallest / len(cuts), top_value / len(cuts))
        return jnp.repeat(jnp.exp(steps), dims[dim] // shards_of).reshape((-1,) + (1,) * (len(dims) - dim - 1))

    gain = one(*cuts[0])
    for cut in cuts[1:]:
        gain = gain * one(*cut)
    return gain


def setup_inputs(seed: int = 0) -> dict:
    keys = jax.random.split(jax.random.key(seed), 7)
    return {
        "estimate": jnp.clip(jnp.exp(math.log(2.0) - 1.3862944 * jax.random.uniform(keys[0], (NZ, NY, NX), jnp.float32) ** block_levels(keys[0], (NZ, NY, NX), ((0, 16),), -0.2, 0.2)), 0.5, 2.0),
        "image": draw_image(jax.random.fold_in(keys[6], 71), 0),
        "psf": jnp.clip(jnp.exp(math.log(1.0) - 2.9957323 * jax.random.uniform(keys[2], (VIEWS, 3, TAPS), jnp.float32) ** block_levels(keys[2], (VIEWS, 3, TAPS), ((0, 16),), -0.2, 0.2)), 0.05, 1.0),
        "perm": with_ends(jax.random.randint(keys[3], (VIEWS,), 0, 2), jax.random.fold_in(keys[3], 1), 0, 1).astype(jnp.int32),
        "shift": with_ends(jax.random.randint(keys[4], (VIEWS,), 0 - NY // 4, NY // 4), jax.random.fold_in(keys[4], 1), 0 - NY // 4, (NY // 4) - 1).astype(jnp.int32),
        "visible": with_ends((jax.random.randint(keys[5], (VIEWS, NZ), 0, 3) < 2).astype(jnp.int32), jax.random.fold_in(keys[5], 1), 0, 1),
    }


def blur_axis(values, kernel, axis, cyclic):
    margin = kernel.shape[0] // 2
    widths = [(0, 0)] * values.ndim
    widths[axis] = (margin, margin)
    padded = jnp.pad(values, widths, mode="wrap" if cyclic else "constant")
    extent = values.shape[axis]
    summed = jnp.zeros(values.shape, jnp.float32)
    for offset in range(kernel.shape[0]):
        summed = summed + kernel[offset] * lax.slice_in_dim(padded, offset, offset + extent, axis=axis)
    return summed


def reference(estimate, image, psf, perm, shift, visible):
    def one_view(log_total, inputs):
        stack, raw_taps, turned, moved, seen = inputs
        kernels = raw_taps / jnp.sum(raw_taps, axis=1, keepdims=True)
        framed = jnp.where(turned == 1, jnp.transpose(estimate, (2, 1, 0)), estimate)
        viewed = jnp.roll(framed, moved, axis=1)
        blurred = blur_axis(blur_axis(blur_axis(viewed, kernels[0], 0, False), kernels[1], 1, True), kernels[2], 2, False)
        ratio = stack / blurred
        flipped = kernels[:, ::-1]
        correction = blur_axis(blur_axis(blur_axis(ratio, flipped[2], 2, False), flipped[1], 1, True), flipped[0], 0, False)
        unrolled = jnp.roll(correction, -moved, axis=1)
        joined = jnp.where(turned == 1, jnp.transpose(unrolled, (2, 1, 0)), unrolled)
        weight = jnp.where(seen == 1, 1.0, 0.0).astype(jnp.float32)
        return log_total + weight[:, None, None] * jnp.log(joined), None

    log_total, unused = lax.scan(one_view, jnp.zeros(estimate.shape, jnp.float32), (image, psf, perm, shift, visible))
    return estimate * jnp.exp(log_total / VIEWS)
```

```python
import jax
import jax.numpy as jnp
from jax import lax
from jax.experimental import pallas as pl
from jax.experimental.pallas import tpu as pltpu
from jax.sharding import PartitionSpec as P

MESH = pl.DeviceIdType.MESH
F32 = jnp.float32
BF16 = jnp.bfloat16
PIECE = 33 * 8


def split(x):
    high = x.astype(BF16)
    return high, (x - high.astype(F32)).astype(BF16)


def dot3(ah, al, bh, bl):
    def dot(a, b):
        return lax.dot_general(a, b, (((1,), (0,)), ((), ())), preferred_element_type=F32)

    return dot(ah, bh) + dot(ah, bl) + dot(al, bh)


def lane_groups(ins):
    group = lax.broadcasted_iota(jnp.int32, (8, 128), 1) >> 5
    outs = []
    for i in range(4):
        out = ins[i]
        for j in range(4):
            if j != i:
                out = jnp.where(group == j, pltpu.roll(ins[j], (32 * (j - i)) % 128, 1), out)
        outs.append(out)
    return outs


def make_messages(load, box):
    for half in range(2):
        stacked = jnp.concatenate([load(half, c) for c in range(4)], axis=0)
        turned = stacked.T
        for r in range(4):
            outs = lane_groups([turned[r * 32 + q * 8 : r * 32 + q * 8 + 8] for q in range(4)])
            for c in range(4):
                box[4 * c + r, half] = outs[c]


def take_messages(box, piece):
    for half in range(2):
        for c in range(4):
            outs = lane_groups([box[4 * c + r, half] for r in range(4)])
            for q in range(4):
                piece[pl.ds(q * 64 + half * 4 + c, 8, stride=8), :] = outs[q]


def kernel(
    psf, perm, shift, visible, e_hbm, i_hbm, o_hbm,
    ec, image, f, fh, fl, r, mfh, mfl, mah, mal, tfh, tfl, tah, tal,
    sbox, rbox, sbox2, rbox2, visrow, epiece, piece, gathered, lp, rb, upiece, tpiece, ttpiece, gathered2, result,
    local_sem, a1s, a1r, a2s, a2r, g1s, g1r, g1f, g2s, g2r, g2f, hs, hr, rs, rr,
):
    v = lax.axis_index("view")
    b = lax.axis_index("bulk")
    core = v % 2
    chip = v // 2

    loads = [
        pltpu.make_async_copy(e_hbm.at[:, :, pl.ds(128 * c, 128)], ec.at[c], local_sem.at[c])
        for c in range(4)
    ]
    image_load = pltpu.make_async_copy(i_hbm.at[0], image, local_sem.at[4])
    for load in loads:
        load.start()
    image_load.start()

    barrier = pltpu.get_barrier_semaphore()

    @pl.loop(1, 16)
    def _(d):
        pl.semaphore_signal(barrier, inc=1, device_id=((v + d) % 16, b), device_id_type=MESH)
        pl.semaphore_signal(barrier, inc=1, device_id=(v, (b + d) % 16), device_id_type=MESH)

    turned = perm[0] == 1
    moved = shift[0]

    row = lax.broadcasted_iota(jnp.int32, (32, 128), 0)
    lane = lax.broadcasted_iota(jnp.int32, (32, 128), 1)

    def pick(index, axis, reverse, shape):
        total = psf[0, axis, 0]
        for t in range(1, 15):
            total = total + psf[0, axis, t]
        out = jnp.zeros(shape, F32)
        for t in range(15):
            out = jnp.where(index == t, psf[0, axis, 14 - t if reverse else t], out)
        return out / jnp.full(shape, total, F32)

    zlane = lax.broadcasted_iota(jnp.int32, (8, 768), 1) >> 5
    brow = lax.broadcasted_iota(jnp.int32, (128, 128), 0)
    blane = lax.broadcasted_iota(jnp.int32, (128, 128), 1)
    for reverse, mh, ml, th, tl in ((False, mfh, mfl, tfh, tfl), (True, mah, mal, tah, tal)):
        offset = -moved if reverse else moved
        circ = pick(((lane & 31) - row + 7 + offset) & 31, 1, reverse, (32, 128))
        wide = jnp.concatenate([circ] * 6, axis=1)
        for zo in range(8):
            zrow = pick(zlane - zo - 1, 0, reverse, (8, 768))
            high, low = split(wide * zrow[0:1])
            mh[zo * 32 : zo * 32 + 32, :] = high
            ml[zo * 32 : zo * 32 + 32, :] = low
        th[...] = jnp.zeros((512, 512), BF16)
        tl[...] = jnp.zeros((512, 512), BF16)
        for delta in (-1, 0, 1):
            high, low = split(pick(brow - blane - 128 * delta + 7, 2, reverse, (128, 128)))
            for i in range(4):
                j = i + delta
                if 0 <= j < 4:
                    th[i * 128 : i * 128 + 128, j * 128 : j * 128 + 128] = high
                    tl[i * 128 : i * 128 + 128, j * 128 : j * 128 + 128] = low

    vlane = lax.broadcasted_iota(jnp.int32, (8, 128), 1) & 31
    vtile = jnp.zeros((8, 128), F32)
    for t in range(32):
        vtile = jnp.where(vlane == t, jnp.where(visible[0, t] == 1, 1.0, 0.0), vtile)

    for load in loads:
        load.wait()

    erows_flat = ec.reshape(4 * 1024, 128)

    def erows(half, c):
        return erows_flat[pl.ds(1024 * c + v + 16 * half, 32, stride=32), :]

    for half in range(2):
        for c in range(4):
            epiece[pl.ds(half * 4 + c, 32, stride=8), :] = erows(half, c)
    make_messages(erows, sbox)
    for t in range(16):
        sbox[t, 2] = vtile

    for ref in (f, r):
        zero = jnp.zeros((32, 512), F32)
        ref[0] = zero
        ref[47] = zero

        @pl.when(b == 0)
        def _():
            for t in range(1, 8):
                ref[t] = zero

        @pl.when(b == 15)
        def _():
            for t in range(40, 47):
                ref[t] = zero

    pl.semaphore_wait(barrier, 30)

    def exchange(source, target, send, recv):
        @pl.loop(1, 16)
        def _(d):
            other = (b + d) % 16
            pltpu.make_async_remote_copy(
                source.at[other], target.at[b], send.at[other], recv.at[b],
                device_id=(v, other), device_id_type=MESH,
            ).start()

        target[b] = source[b]

        @pl.loop(1, 16)
        def _(d):
            other = (b + d) % 16
            copy = pltpu.make_async_remote_copy(
                source.at[other], target.at[other], send.at[other], recv.at[other],
                device_id=(v, other), device_id_type=MESH,
            )
            copy.wait_send()
            copy.wait_recv()

    exchange(sbox, rbox, a1s, a1r)
    take_messages(rbox, piece)
    group = lax.broadcasted_iota(jnp.int32, (8, 128), 1) >> 5
    for c in range(4):
        seen = rbox[4 * c, 2]
        for q in range(1, 4):
            seen = jnp.where(group == q, rbox[4 * c + q, 2], seen)
        visrow[:, 128 * c : 128 * c + 128] = seen

    def gather(own, everything, send, recv, forward):
        sibling = v + 1 - 2 * core
        direct = pltpu.make_async_remote_copy(
            own, everything.at[v], send.at[8], recv.at[v], device_id=(sibling, b), device_id_type=MESH
        )
        direct.start()

        @pl.loop(1, 8)
        def _(d):
            other = ((chip + d) % 8) * 2 + core
            pltpu.make_async_remote_copy(
                own, everything.at[v], send.at[d], recv.at[v], device_id=(other, b), device_id_type=MESH
            ).start()

        @pl.loop(0, 32)
        def _(t):
            rows = pl.ds(pl.multiple_of(t * 8, 8), 8)
            everything.at[v][rows, :] = own[rows, :]

        @pl.loop(1, 8)
        def _(d):
            other = ((chip + 8 - d) % 8) * 2 + core
            landed = everything.at[other]
            pltpu.make_async_remote_copy(
                own, landed, send.at[d], recv.at[other], device_id=(other, b), device_id_type=MESH
            ).wait_recv()
            pltpu.make_async_remote_copy(
                landed, landed, forward.at[d], recv.at[other], device_id=(sibling, b), device_id_type=MESH
            ).start()

        @pl.loop(0, 8)
        def _(d):
            other = ((chip + 8 - d) % 8) * 2 + 1 - core
            pltpu.make_async_remote_copy(
                own, everything.at[other], send.at[8], recv.at[other], device_id=(sibling, b), device_id_type=MESH
            ).wait_recv()

        direct.wait_send()

        @pl.loop(1, 8)
        def _(d):
            for sem in (send, forward):
                pltpu.make_async_remote_copy(
                    own, everything.at[v], sem.at[d], recv.at[v], device_id=(sibling, b), device_id_type=MESH
                ).wait_send()

    gather(piece, gathered, g1s, g1r, g1f)

    flat = gathered.reshape(16 * 256, 128)

    @pl.loop(0, 32)
    def _(x):
        for t in range(4):
            for c in range(4):
                start = (8 * (t % 2)) * 256 + x * 8 + (t // 2) * 4 + c
                swapped = flat[pl.ds(start, 8, stride=256), :]
                own = ec[c, x, 8 * t : 8 * t + 8, :]
                f[x + 8, 8 * t : 8 * t + 8, 128 * c : 128 * c + 128] = jnp.where(turned, swapped, own)

    def halo(ref, base):
        low = pltpu.make_async_remote_copy(
            ref.at[pl.ds(8, 7)], ref.at[pl.ds(40, 7)], hs.at[base], hr.at[base],
            device_id=(v, (b + 15) % 16), device_id_type=MESH,
        )
        high = pltpu.make_async_remote_copy(
            ref.at[pl.ds(33, 7)], ref.at[pl.ds(1, 7)], hs.at[base + 1], hr.at[base + 1],
            device_id=(v, (b + 1) % 16), device_id_type=MESH,
        )

        @pl.when(b > 0)
        def _():
            low.start()

        @pl.when(b < 15)
        def _():
            high.start()

        @pl.when(b > 0)
        def _():
            low.wait_send()
            high.wait_recv()

        @pl.when(b < 15)
        def _():
            high.wait_send()
            low.wait_recv()

    def split_rows(ref):
        @pl.loop(0, 48)
        def _(t):
            rows = pl.ds(pl.multiple_of(t * 32, 32), 32)
            high, low = split(ref[t])
            fh[rows, :] = high
            fl[rows, :] = low

    halo(f, 0)
    split_rows(f)
    image_load.wait()

    @pl.loop(0, 4)
    def _(g):
        rows = pl.ds(pl.multiple_of(g * 256, 256), 768)
        high, low = split(dot3(mfh[...], mfl[...], fh[rows, :], fl[rows, :]))
        blurred = dot3(high, low, tfh[...], tfl[...])
        ratio = image[pl.ds(8 * g, 8)] / blurred.reshape(8, 32, 512)
        r[pl.ds(8 * g + 8, 8)] = ratio

    halo(r, 2)
    split_rows(r)

    lflat = lp.reshape(16 * PIECE, 128)

    @pl.loop(0, 4)
    def _(g):
        rows = pl.ds(pl.multiple_of(g * 256, 256), 768)
        high, low = split(dot3(mah[...], mal[...], fh[rows, :], fl[rows, :]))
        result[pl.ds(8 * g, 8)] = dot3(high, low, tah[...], tal[...]).reshape(8, 32, 512)

    @pl.loop(0, 32)
    def _(z):
        seen = jnp.where(visible[0, z] == 1, 1.0, 0.0)
        for c in range(4):
            weight = jnp.where(turned, visrow[:, 128 * c : 128 * c + 128], jnp.full((8, 128), seen, F32))
            for t in range(4):
                term = weight * jnp.log(result[z, 8 * t : 8 * t + 8, 128 * c : 128 * c + 128])
                start = (8 * (t % 2)) * PIECE + z * 8 + (t // 2) * 4 + c
                lflat[pl.ds(start, 8, stride=PIECE), :] = term

    flag = jnp.full((8, 128), jnp.where(turned, 1.0, 0.0), F32)
    for w in range(16):
        lp[w, 256:264, :] = flag

    @pl.loop(1, 16)
    def _(d):
        other = (v + d) % 16
        pltpu.make_async_remote_copy(
            lp.at[other], rb.at[v], rs.at[other], rr.at[v], device_id=(other, b), device_id_type=MESH
        ).start()

    @pl.loop(0, 33)
    def _(t):
        rows = pl.ds(pl.multiple_of(t * 8, 8), 8)
        rb.at[v][rows, :] = lp.at[v][rows, :]

    @pl.loop(1, 16)
    def _(d):
        other = (v + d) % 16
        copy = pltpu.make_async_remote_copy(
            lp.at[other], rb.at[other], rs.at[other], rr.at[other], device_id=(other, b), device_id_type=MESH
        )
        copy.wait_send()
        copy.wait_recv()

    @pl.loop(0, 32)
    def _(z):
        rows = pl.ds(pl.multiple_of(z * 8, 8), 8)
        up = jnp.zeros((8, 128), F32)
        tp = jnp.zeros((8, 128), F32)
        for w in range(16):
            term = rb[w, rows, :]
            share = term * rb[w, 256:264, :]
            tp = tp + share
            up = up + (term - share)
        upiece[rows, :] = up
        tpiece[rows, :] = tp

    make_messages(lambda half, c: tpiece[pl.ds(half * 4 + c, 32, stride=8), :], sbox2)
    exchange(sbox2, rbox2, a2s, a2r)
    take_messages(rbox2, ttpiece)
    upiece[...] = epiece[...] * jnp.exp((upiece[...] + ttpiece[...]) * (1.0 / 16.0))
    gather(upiece, gathered2, g2s, g2r, g2f)

    flat2 = gathered2.reshape(16 * 256, 128)

    @pl.loop(0, 32)
    def _(x):
        for t in range(4):
            for c in range(4):
                start = (8 * (t % 2)) * 256 + x * 8 + (t // 2) * 4 + c
                result[x, 8 * t : 8 * t + 8, 128 * c : 128 * c + 128] = flat2[pl.ds(start, 8, stride=256), :]

    done = pltpu.make_async_copy(result, o_hbm, local_sem.at[0])
    done.start()
    done.wait()


def shards(estimate, image, psf, perm, shift, visible):
    smem = pl.BlockSpec(memory_space=pltpu.SMEM)
    hbm = pl.BlockSpec(memory_space=pl.ANY)
    vmem = pltpu.VMEM
    dma = pltpu.SemaphoreType.DMA
    return pl.pallas_call(
        kernel,
        out_shape=jax.ShapeDtypeStruct(estimate.shape, F32),
        in_specs=[smem] * 4 + [hbm] * 2,
        out_specs=hbm,
        scratch_shapes=[
            vmem((4, 32, 32, 128), F32),
            vmem((32, 32, 512), F32),
            vmem((48, 32, 512), F32),
            vmem((1536, 512), BF16),
            vmem((1536, 512), BF16),
            vmem((48, 32, 512), F32),
            vmem((256, 768), BF16),
            vmem((256, 768), BF16),
            vmem((256, 768), BF16),
            vmem((256, 768), BF16),
            vmem((512, 512), BF16),
            vmem((512, 512), BF16),
            vmem((512, 512), BF16),
            vmem((512, 512), BF16),
            vmem((16, 3, 8, 128), F32),
            vmem((16, 3, 8, 128), F32),
            vmem((16, 2, 8, 128), F32),
            vmem((16, 2, 8, 128), F32),
            vmem((8, 512), F32),
            vmem((256, 128), F32),
            vmem((256, 128), F32),
            vmem((16, 256, 128), F32),
            vmem((16, PIECE, 128), F32),
            vmem((16, PIECE, 128), F32),
            vmem((256, 128), F32),
            vmem((256, 128), F32),
            vmem((256, 128), F32),
            vmem((16, 256, 128), F32),
            vmem((32, 32, 512), F32),
            dma((5,)),
            dma((16,)),
            dma((16,)),
            dma((16,)),
            dma((16,)),
            dma((9,)),
            dma((16,)),
            dma((8,)),
            dma((9,)),
            dma((16,)),
            dma((8,)),
            dma((4,)),
            dma((4,)),
            dma((16,)),
            dma((16,)),
        ],
        compiler_params=pltpu.CompilerParams(
            collective_id=0, has_side_effects=True, vmem_limit_bytes=60 * 1024 * 1024
        ),
    )(psf, perm, shift, visible, estimate, image)


def solution(mesh):
    placed = (
        P("bulk", None, None),
        P("view", "bulk", None, None),
        P("view", None, None),
        P("view"),
        P("view"),
        P("view", "bulk"),
    )
    return jax.shard_map(
        shards, mesh=mesh, in_specs=placed, out_specs=P("bulk", None, None), check_vma=False
    )
```

```python
import jax
import jax.numpy as jnp
from jax import lax
from jax.experimental import pallas as pl
from jax.experimental.pallas import tpu as pltpu
from jax.sharding import PartitionSpec as P

MESH = pl.DeviceIdType.MESH
F32 = jnp.float32
BF16 = jnp.bfloat16
PIECE = 33 * 8


def split(x):
    high = x.astype(BF16)
    return high, (x - high.astype(F32)).astype(BF16)


def dot3(ah, al, bh, bl):
    def dot(a, b):
        return lax.dot_general(a, b, (((1,), (0,)), ((), ())), preferred_element_type=F32)

    return dot(ah, bh) + dot(ah, bl) + dot(al, bh)


def lane_groups(ins):
    group = lax.broadcasted_iota(jnp.int32, (8, 128), 1) >> 5
    outs = []
    for i in range(4):
        out = ins[i]
        for j in range(4):
            if j != i:
                out = jnp.where(group == j, pltpu.roll(ins[j], (32 * (j - i)) % 128, 1), out)
        outs.append(out)
    return outs


def make_messages(load, box):
    for half in range(2):
        stacked = jnp.concatenate([load(half, c) for c in range(4)], axis=0)
        turned = stacked.T
        for r in range(4):
            outs = lane_groups([turned[r * 32 + q * 8 : r * 32 + q * 8 + 8] for q in range(4)])
            for c in range(4):
                box[4 * c + r, half] = outs[c]


def take_messages(box, piece):
    for half in range(2):
        for c in range(4):
            outs = lane_groups([box[4 * c + r, half] for r in range(4)])
            for q in range(4):
                piece[pl.ds(q * 64 + half * 4 + c, 8, stride=8), :] = outs[q]


ORDER = (
    (1, 0, 0), (3, 0, 0), (0, 1, 0), (1, 0, 1), (3, 0, 1), (0, 1, 1), (2, 0, 0), (1, 1, 0),
    (3, 1, 0), (2, 0, 1), (1, 1, 1), (3, 1, 1), (2, 1, 0), (2, 1, 1), (0, 0, 1),
)


def kernel(
    psf_hbm, perm, shift, visible, e_hbm, i_hbm, o_hbm,
    psf, ec, image, eh, tedge, fh, fl, rh, rl, redge, rhalo, mfh, mfl, mah, mal, tfh, tfl, tah, tal,
    sbox, rbox, sbox2, rbox2, visrow, epiece, piece, gathered, correction, lp, rb,
    upiece, tpiece, ttpiece, gathered2, result,
    local_sem, a1s, a1r, a2s, a2r, g1s, g1r, g1f, g2s, g2r, g2f, es, er, ef, ts, tr, tf, hs, hr, rs, rr,
):
    v = lax.axis_index("view")
    b = lax.axis_index("bulk")
    core = v % 2
    chip = v // 2
    sibling = v + 1 - 2 * core

    psf_load = pltpu.make_async_copy(psf_hbm, psf, local_sem.at[5])
    psf_load.start()
    loads = [
        pltpu.make_async_copy(e_hbm.at[:, :, pl.ds(128 * c, 128)], ec.at[c], local_sem.at[c])
        for c in range(4)
    ]
    image_load = pltpu.make_async_copy(i_hbm.at[0], image, local_sem.at[4])
    for load in loads:
        load.start()
    image_load.start()

    barrier = pltpu.get_barrier_semaphore()

    @pl.loop(1, 16)
    def _(d):
        pl.semaphore_signal(barrier, inc=1, device_id=((v + d) % 16, b), device_id_type=MESH)
        pl.semaphore_signal(barrier, inc=1, device_id=(v, (b + d) % 16), device_id_type=MESH)

    turned = perm[0] == 1
    moved = shift[0]
    psf_load.wait()

    row = lax.broadcasted_iota(jnp.int32, (32, 128), 0)
    lane = lax.broadcasted_iota(jnp.int32, (32, 128), 1)

    def pick(index, axis, reverse, shape):
        total = psf[0, axis, 0]
        for t in range(1, 15):
            total = total + psf[0, axis, t]
        out = jnp.zeros(shape, F32)
        for t in range(15):
            out = jnp.where(index == t, psf[0, axis, 14 - t if reverse else t], out)
        return out / jnp.full(shape, total, F32)

    zlane = lax.broadcasted_iota(jnp.int32, (8, 768), 1) >> 5
    brow = lax.broadcasted_iota(jnp.int32, (128, 128), 0)
    blane = lax.broadcasted_iota(jnp.int32, (128, 128), 1)
    for reverse, mh, ml, th, tl in ((False, mfh, mfl, tfh, tfl), (True, mah, mal, tah, tal)):
        offset = -moved if reverse else moved
        circ = pick(((lane & 31) - row + 7 + offset) & 31, 1, reverse, (32, 128))
        wide = jnp.concatenate([circ] * 6, axis=1)
        for zo in range(8):
            zrow = pick(zlane - zo - 1, 0, reverse, (8, 768))
            high, low = split(wide * zrow[0:1])
            mh[zo * 32 : zo * 32 + 32, :] = high
            ml[zo * 32 : zo * 32 + 32, :] = low
        th[...] = jnp.zeros((512, 512), BF16)
        tl[...] = jnp.zeros((512, 512), BF16)
        for delta in (-1, 0, 1):
            high, low = split(pick(brow - blane - 128 * delta + 7, 2, reverse, (128, 128)))
            for i in range(4):
                j = i + delta
                if 0 <= j < 4:
                    th[i * 128 : i * 128 + 128, j * 128 : j * 128 + 128] = high
                    tl[i * 128 : i * 128 + 128, j * 128 : j * 128 + 128] = low

    vlane = lax.broadcasted_iota(jnp.int32, (8, 128), 1) & 31
    vtile = jnp.zeros((8, 128), F32)
    for t in range(32):
        vtile = jnp.where(vlane == t, jnp.where(visible[0, t] == 1, 1.0, 0.0), vtile)

    for load in loads:
        load.wait()

    erows_flat = ec.reshape(4 * 1024, 128)

    def erows(half, c):
        return erows_flat[pl.ds(1024 * c + v + 16 * half, 32, stride=32), :]

    for half in range(2):
        for c in range(4):
            epiece[pl.ds(half * 4 + c, 32, stride=8), :] = erows(half, c)
    make_messages(erows, sbox)
    for t in range(16):
        sbox[t, 2] = vtile

    zero = jnp.zeros((32, 512), BF16)
    for ref in (fh, fl, rh, rl):
        ref[0:32, :] = zero
        ref[1504:1536, :] = zero

        @pl.when(b == 0)
        def _():
            for t in range(1, 8):
                ref[t * 32 : t * 32 + 32, :] = zero

        @pl.when(b == 15)
        def _():
            for t in range(40, 47):
                ref[t * 32 : t * 32 + 32, :] = zero

    pl.semaphore_wait(barrier, 30)

    def exchange(source, target, send, recv):
        @pl.loop(1, 16)
        def _(d):
            other = (b + d) % 16
            pltpu.make_async_remote_copy(
                source.at[other], target.at[b], send.at[other], recv.at[b],
                device_id=(v, other), device_id_type=MESH,
            ).start()

        target[b] = source[b]

        @pl.loop(1, 16)
        def _(d):
            other = (b + d) % 16
            copy = pltpu.make_async_remote_copy(
                source.at[other], target.at[other], send.at[other], recv.at[other],
                device_id=(v, other), device_id_type=MESH,
            )
            copy.wait_send()
            copy.wait_recv()

    exchange(sbox, rbox, a1s, a1r)

    after = b + 1 - 2 * core
    before = b - 1 + 2 * core
    has_after = (after >= 0) & (after < 16)
    has_before = (before >= 0) & (before < 16)
    edge = pltpu.make_async_remote_copy(
        e_hbm.at[pl.ds(25 * (1 - core), 7)], eh.at[core], es, er.at[0], device_id=(v, (after + 16) % 16), device_id_type=MESH
    )

    @pl.when(has_after)
    def _():
        edge.start()

    take_messages(rbox, piece)
    group = lax.broadcasted_iota(jnp.int32, (8, 128), 1) >> 5
    for c in range(4):
        seen = rbox[4 * c, 2]
        for q in range(1, 4):
            seen = jnp.where(group == q, rbox[4 * c + q, 2], seen)
        visrow[:, 128 * c : 128 * c + 128] = seen

    def gather(own, everything, send, recv, forward, on_piece):
        direct = pltpu.make_async_remote_copy(
            own, everything.at[v], send.at[8], recv.at[v], device_id=(sibling, b), device_id_type=MESH
        )
        for d in (1, 7, 4, 2, 5, 3, 6):
            other = ((chip + d) % 8) * 2 + core
            pltpu.make_async_remote_copy(
                own, everything.at[v], send.at[d], recv.at[v], device_id=(other, b), device_id_type=MESH
            ).start()
        direct.start()
        on_piece(0, own, v)

        @pl.loop(0, 32)
        def _(t):
            rows = pl.ds(pl.multiple_of(t * 8, 8), 8)
            everything.at[v][rows, :] = own[rows, :]

        for d in (1, 7, 4, 2, 5, 3, 6):
            other = ((chip + 8 - d) % 8) * 2 + core
            landed = everything.at[other]
            pltpu.make_async_remote_copy(
                own, landed, send.at[d], recv.at[other], device_id=(other, b), device_id_type=MESH
            ).wait_recv()
            pltpu.make_async_remote_copy(
                landed, landed, forward.at[d], recv.at[other], device_id=(sibling, b), device_id_type=MESH
            ).start()
            on_piece(d, landed, other)

        @pl.loop(0, 8)
        def _(d):
            other = ((chip + 8 - d) % 8) * 2 + 1 - core
            pltpu.make_async_remote_copy(
                own, everything.at[other], send.at[8], recv.at[other], device_id=(sibling, b), device_id_type=MESH
            ).wait_recv()

        direct.wait_send()

        @pl.loop(1, 8)
        def _(d):
            for sem in (send, forward):
                pltpu.make_async_remote_copy(
                    own, everything.at[v], sem.at[d], recv.at[v], device_id=(sibling, b), device_id_type=MESH
                ).wait_send()

    def edge_copy(d, ref, w, slot):
        return pltpu.make_async_remote_copy(
            ref.at[pl.ds(200 * (1 - slot), 56)], tedge.at[w, slot], ts.at[d, slot], tr.at[w, slot],
            device_id=(v, (b + 17 - 2 * slot) % 16), device_id_type=MESH,
        )

    def send_edges(d, ref, w):
        @pl.when(b < 15)
        def _():
            edge_copy(d, ref, w, 0).start()

        @pl.when(b > 0)
        def _():
            edge_copy(d, ref, w, 1).start()

    gather(piece, gathered, g1s, g1r, g1f, send_edges)

    edge_pass = pltpu.make_async_remote_copy(
        eh.at[core], eh.at[core], ef, er.at[1], device_id=(sibling, b), device_id_type=MESH
    )

    @pl.when(has_before)
    def _():
        edge.wait_recv()
        edge_pass.start()

    @pl.when(has_after)
    def _():
        edge.wait_send()

    def pass_copy(d, w, slot):
        return pltpu.make_async_remote_copy(
            tedge.at[w, slot], tedge.at[w, slot], tf.at[d, slot], tr.at[w, slot],
            device_id=(sibling, b), device_id_type=MESH,
        )

    for slot in range(2):
        here = b > 0 if slot == 0 else b < 15
        there = b < 15 if slot == 0 else b > 0

        @pl.when(here)
        def _():
            for d in (0, 1, 7, 4, 2, 5, 3, 6):
                w = ((chip + 8 - d) % 8) * 2 + core
                edge_copy(d, piece, w, slot).wait_recv()
                pass_copy(d, w, slot).start()

        @pl.when(there)
        def _():
            for d in range(8):
                edge_copy(d, piece, v, slot).wait_send()

    flat = gathered.reshape(16 * 256, 128)

    def put(plane, half, c, value):
        rows = pl.ds(pl.multiple_of(plane * 32 + 16 * half, 16), 16)
        high, low = split(value)
        fh[rows, 128 * c : 128 * c + 128] = high
        fl[rows, 128 * c : 128 * c + 128] = low

    @pl.loop(0, 32)
    def _(x):
        for half in range(2):
            for c in range(4):
                swapped = jnp.concatenate(
                    [flat[pl.ds(t * 2048 + x * 8 + half * 4 + c, 8, stride=256), :] for t in range(2)], axis=0
                )
                put(x + 8, half, c, jnp.where(turned, swapped, ec[c, x, 16 * half : 16 * half + 16, :]))

    edge_flat = tedge.reshape(16 * 112, 128)

    @pl.when(has_before)
    def _():
        edge_pass.wait_send()

    @pl.when(has_after)
    def _():
        pltpu.make_async_remote_copy(
            eh.at[1 - core], eh.at[1 - core], ef, er.at[1], device_id=(sibling, b), device_id_type=MESH
        ).wait_recv()

    for slot in range(2):
        here = b > 0 if slot == 0 else b < 15

        @pl.when(here)
        def _():
            for d in range(8):
                w = ((chip + 8 - d) % 8) * 2 + core
                pass_copy(d, w, slot).wait_send()
                pass_copy(d, ((chip + 8 - d) % 8) * 2 + 1 - core, slot).wait_recv()

            @pl.loop(0, 7)
            def _(x):
                for half in range(2):
                    for c in range(4):
                        start = slot * 56 + x * 8 + half * 4 + c
                        swapped = jnp.concatenate(
                            [edge_flat[pl.ds(t * 896 + start, 8, stride=112), :] for t in range(2)], axis=0
                        )
                        own = eh[slot, x, 16 * half : 16 * half + 16, 128 * c : 128 * c + 128]
                        put(x + 1 + 39 * slot, half, c, jnp.where(turned, swapped, own))

    image_load.wait()
    low_halo = pltpu.make_async_remote_copy(
        redge.at[pl.ds(0, 7)], rhalo.at[1], hs.at[0], hr.at[0],
        device_id=(v, (b + 15) % 16), device_id_type=MESH,
    )
    high_halo = pltpu.make_async_remote_copy(
        redge.at[pl.ds(9, 7)], rhalo.at[0], hs.at[1], hr.at[1],
        device_id=(v, (b + 1) % 16), device_id_type=MESH,
    )

    @pl.loop(0, 4)
    def _(i):
        g = (3 * i) % 4
        rows = pl.ds(pl.multiple_of(g * 256, 256), 768)
        high, low = split(dot3(mfh[...], mfl[...], fh[rows, :], fl[rows, :]))
        blurred = dot3(high, low, tfh[...], tfl[...])
        ratio = image[pl.ds(8 * g, 8)].reshape(256, 512) / blurred
        high, low = split(ratio)
        inner = pl.ds(pl.multiple_of(g * 256 + 256, 256), 256)
        rh[inner, :] = high
        rl[inner, :] = low

        @pl.when(i < 2)
        def _():
            redge[pl.ds(8 * i, 8)] = ratio.reshape(8, 32, 512)

        @pl.when((i == 0) & (b > 0))
        def _():
            low_halo.start()

        @pl.when((i == 1) & (b < 15))
        def _():
            high_halo.start()

    lflat = lp.reshape(16 * PIECE, 128)
    flag = jnp.full((8, 128), jnp.where(turned, 1.0, 0.0), F32)
    for w in range(16):
        lp[w, 0:8, :] = flag

    def back(g, place):
        rows = pl.ds(pl.multiple_of(g * 256, 256), 768)
        high, low = split(dot3(mah[...], mal[...], rh[rows, :], rl[rows, :]))
        correction[...] = dot3(high, low, tah[...], tal[...]).reshape(8, 32, 512)

        @pl.loop(0, 8)
        def _(k):
            seen = jnp.where(visible[0, g * 8 + k] == 1, 1.0, 0.0)
            for c in range(4):
                weight = jnp.where(turned, visrow[:, 128 * c : 128 * c + 128], jnp.full((8, 128), seen, F32))
                for t in range(4):
                    term = weight * jnp.log(correction[k, 8 * t : 8 * t + 8, 128 * c : 128 * c + 128])
                    start = (8 * (t % 2)) * PIECE + (place + k) * 8 + 8 + (t // 2) * 4 + c
                    lflat[pl.ds(start, 8, stride=PIECE), :] = term

    x = chip % 4
    side = chip // 4

    def direct(part, other, origin):
        rows = pl.ds(0, 136) if part == 0 else pl.ds(136, 128)
        return pltpu.make_async_remote_copy(
            lp.at[other, rows], rb.at[origin, rows], rs.at[part, other], rr.at[part, origin],
            device_id=(other, b), device_id_type=MESH,
        )

    def send_part(part):
        for dx, dy, dc in ORDER:
            other = (side + dy - 2 * dy * side) * 8 + ((x + dx) % 4) * 2 + core + dc - 2 * dc * core
            direct(part, other, v).start()

    @pl.loop(0, 2)
    def _(i):
        back(i + 1, 8 * i)

    send_part(0)

    def take_halo(slot):
        @pl.loop(0, 7)
        def _(t):
            high, low = split(rhalo[slot, t])
            rows = pl.ds(pl.multiple_of((t + 1 + 39 * slot) * 32, 32), 32)
            rh[rows, :] = high
            rl[rows, :] = low

    @pl.when(b > 0)
    def _():
        low_halo.wait_send()
        high_halo.wait_recv()
        take_halo(0)

    @pl.when(b < 15)
    def _():
        high_halo.wait_send()
        low_halo.wait_recv()
        take_halo(1)

    @pl.loop(0, 2)
    def _(i):
        back(3 * i, 16 + 8 * i)

    send_part(1)

    def sums(z, place):
        rows = pl.ds(pl.multiple_of(place * 8 + 8, 8), 8)
        up = jnp.zeros((8, 128), F32)
        tp = jnp.zeros((8, 128), F32)
        for w in range(16):
            term = rb[w, rows, :]
            share = term * rb[w, 0:8, :]
            tp = tp + share
            up = up + (term - share)
        rows = pl.ds(pl.multiple_of(z * 8, 8), 8)
        upiece[rows, :] = up
        tpiece[rows, :] = tp

    def take_part(part):
        @pl.loop(0, 17 - part)
        def _(t):
            rows = pl.ds(pl.multiple_of(t * 8 + 136 * part, 8), 8)
            rb.at[v][rows, :] = lp.at[v][rows, :]

        @pl.loop(1, 16)
        def _(d):
            other = (v + d) % 16
            direct(part, other, other).wait_recv()

    take_part(0)

    @pl.loop(0, 16)
    def _(t):
        sums(t + 8, t)

    take_part(1)

    @pl.loop(0, 16)
    def _(t):
        sums(t + 16 * (t // 8), t + 16)

    for part in range(2):
        @pl.loop(1, 16)
        def _(d):
            other = (v + d) % 16
            direct(part, other, other).wait_send()

    make_messages(lambda half, c: tpiece[pl.ds(half * 4 + c, 32, stride=8), :], sbox2)
    exchange(sbox2, rbox2, a2s, a2r)
    take_messages(rbox2, ttpiece)
    upiece[...] = epiece[...] * jnp.exp((upiece[...] + ttpiece[...]) * (1.0 / 16.0))
    gather(upiece, gathered2, g2s, g2r, g2f, lambda d, ref, w: None)

    flat2 = gathered2.reshape(16 * 256, 128)

    @pl.loop(0, 32)
    def _(x):
        for t in range(4):
            for c in range(4):
                start = (8 * (t % 2)) * 256 + x * 8 + (t // 2) * 4 + c
                result[x, 8 * t : 8 * t + 8, 128 * c : 128 * c + 128] = flat2[pl.ds(start, 8, stride=256), :]

    done = pltpu.make_async_copy(result, o_hbm, local_sem.at[0])
    done.start()
    done.wait()


def shards(estimate, image, psf, perm, shift, visible):
    smem = pl.BlockSpec(memory_space=pltpu.SMEM)
    hbm = pl.BlockSpec(memory_space=pl.ANY)
    vmem = pltpu.VMEM
    dma = pltpu.SemaphoreType.DMA
    return pl.pallas_call(
        kernel,
        out_shape=jax.ShapeDtypeStruct(estimate.shape, F32),
        in_specs=[hbm] + [smem] * 3 + [hbm] * 2,
        out_specs=hbm,
        scratch_shapes=[
            pltpu.SMEM((1, 3, 15), F32),
            vmem((4, 32, 32, 128), F32),
            vmem((32, 32, 512), F32),
            vmem((2, 7, 32, 512), F32),
            vmem((16, 2, 56, 128), F32),
        ]
        + [vmem((1536, 512), BF16)] * 4
        + [vmem((16, 32, 512), F32), vmem((2, 7, 32, 512), F32)]
        + [vmem((256, 768), BF16)] * 4
        + [vmem((512, 512), BF16)] * 4
        + [
            vmem((16, 3, 8, 128), F32),
            vmem((16, 3, 8, 128), F32),
            vmem((16, 2, 8, 128), F32),
            vmem((16, 2, 8, 128), F32),
            vmem((8, 512), F32),
            vmem((256, 128), F32),
            vmem((256, 128), F32),
            vmem((16, 256, 128), F32),
            vmem((8, 32, 512), F32),
            vmem((16, PIECE, 128), F32),
            vmem((16, PIECE, 128), F32),
            vmem((256, 128), F32),
            vmem((256, 128), F32),
            vmem((256, 128), F32),
            vmem((16, 256, 128), F32),
            vmem((32, 32, 512), F32),
            dma((6,)),
        ]
        + [dma((16,))] * 4
        + [dma((9,)), dma((16,)), dma((8,))] * 2
        + [dma, dma((2,)), dma]
        + [dma((8, 2)), dma((16, 2)), dma((8, 2))]
        + [dma((2,)), dma((2,)), dma((2, 16)), dma((2, 16))],
        compiler_params=pltpu.CompilerParams(
            collective_id=0, has_side_effects=True, vmem_limit_bytes=60 * 1024 * 1024
        ),
    )(psf, perm, shift, visible, estimate, image)


def solution(mesh):
    placed = (
        P("bulk", None, None),
        P("view", "bulk", None, None),
        P("view", None, None),
        P("view"),
        P("view"),
        P("view", "bulk"),
    )
    return jax.shard_map(
        shards, mesh=mesh, in_specs=placed, out_specs=P("bulk", None, None), check_vma=False
    )
```

```python
import jax
import jax.numpy as jnp
from jax import lax
from jax.experimental import pallas as pl
from jax.experimental.pallas import tpu as pltpu
from jax.sharding import PartitionSpec as P

MESH = pl.DeviceIdType.MESH
F32 = jnp.float32
BF16 = jnp.bfloat16
PIECE = 33 * 8


def split(x):
    high = x.astype(BF16)
    return high, (x - high.astype(F32)).astype(BF16)


def dot3(ah, al, bh, bl):
    def dot(a, b):
        return lax.dot_general(a, b, (((1,), (0,)), ((), ())), preferred_element_type=F32)

    return dot(ah, bh) + dot(ah, bl) + dot(al, bh)


def lane_groups(ins):
    group = lax.broadcasted_iota(jnp.int32, (8, 128), 1) >> 5
    outs = []
    for i in range(4):
        out = ins[i]
        for j in range(4):
            if j != i:
                out = jnp.where(group == j, pltpu.roll(ins[j], (32 * (j - i)) % 128, 1), out)
        outs.append(out)
    return outs


def make_messages(load, box):
    for half in range(2):
        stacked = jnp.concatenate([load(half, c) for c in range(4)], axis=0)
        turned = stacked.T
        for r in range(4):
            outs = lane_groups([turned[r * 32 + q * 8 : r * 32 + q * 8 + 8] for q in range(4)])
            for c in range(4):
                box[4 * c + r, half] = outs[c]


def take_messages(box, piece):
    for half in range(2):
        for c in range(4):
            outs = lane_groups([box[4 * c + r, half] for r in range(4)])
            for q in range(4):
                piece[pl.ds(q * 64 + half * 4 + c, 8, stride=8), :] = outs[q]


ORDER = (
    (1, 0, 0), (3, 0, 0), (0, 1, 0), (1, 0, 1), (3, 0, 1), (0, 1, 1), (2, 0, 0), (1, 1, 0),
    (3, 1, 0), (2, 0, 1), (1, 1, 1), (3, 1, 1), (2, 1, 0), (2, 1, 1), (0, 0, 1),
)


def kernel(
    psf_hbm, perm, shift, visible, e_hbm, i_hbm, o_hbm,
    psf, ec, image, eh, tedge, fh, fl, rh, rl, redge, rhalo, mfh, mfl, mah, mal, tfh, tfl, tah, tal,
    sbox, rbox, sbox2, rbox2, visrow, epiece, piece, gathered, correction, lp, rb,
    upiece, tpiece, ttpiece, gathered2, result,
    local_sem, a1s, a1r, a2s, a2r, g1s, g1r, g1f, g2s, g2r, g2f, es, er, ef, ts, tr, tf, hs, hr, rs, rr,
):
    v = lax.axis_index("view")
    b = lax.axis_index("bulk")
    core = v % 2
    chip = v // 2
    sibling = v + 1 - 2 * core

    psf_load = pltpu.make_async_copy(psf_hbm, psf, local_sem.at[5])
    psf_load.start()
    loads = [
        pltpu.make_async_copy(e_hbm.at[:, :, pl.ds(128 * c, 128)], ec.at[c], local_sem.at[c])
        for c in range(4)
    ]
    image_load = pltpu.make_async_copy(i_hbm.at[0], image, local_sem.at[4])
    for load in loads:
        load.start()
    image_load.start()

    barrier = pltpu.get_barrier_semaphore()

    @pl.loop(1, 16)
    def _(d):
        pl.semaphore_signal(barrier, inc=1, device_id=((v + d) % 16, b), device_id_type=MESH)
        pl.semaphore_signal(barrier, inc=1, device_id=(v, (b + d) % 16), device_id_type=MESH)

    turned = perm[0] == 1
    moved = shift[0]
    psf_load.wait()

    row = lax.broadcasted_iota(jnp.int32, (32, 128), 0)
    lane = lax.broadcasted_iota(jnp.int32, (32, 128), 1)

    def pick(index, axis, reverse, shape):
        total = psf[0, axis, 0]
        for t in range(1, 15):
            total = total + psf[0, axis, t]
        out = jnp.zeros(shape, F32)
        for t in range(15):
            out = jnp.where(index == t, psf[0, axis, 14 - t if reverse else t], out)
        return out / jnp.full(shape, total, F32)

    zlane = lax.broadcasted_iota(jnp.int32, (8, 768), 1) >> 5
    brow = lax.broadcasted_iota(jnp.int32, (128, 128), 0)
    blane = lax.broadcasted_iota(jnp.int32, (128, 128), 1)
    for reverse, mh, ml, th, tl in ((False, mfh, mfl, tfh, tfl), (True, mah, mal, tah, tal)):
        offset = -moved if reverse else moved
        circ = pick(((lane & 31) - row + 7 + offset) & 31, 1, reverse, (32, 128))
        wide = jnp.concatenate([circ] * 6, axis=1)
        for zo in range(8):
            zrow = pick(zlane - zo - 1, 0, reverse, (8, 768))
            high, low = split(wide * zrow[0:1])
            mh[zo * 32 : zo * 32 + 32, :] = high
            ml[zo * 32 : zo * 32 + 32, :] = low
        th[...] = jnp.zeros((512, 512), BF16)
        tl[...] = jnp.zeros((512, 512), BF16)
        for delta in (-1, 0, 1):
            high, low = split(pick(brow - blane - 128 * delta + 7, 2, reverse, (128, 128)))
            for i in range(4):
                j = i + delta
                if 0 <= j < 4:
                    th[i * 128 : i * 128 + 128, j * 128 : j * 128 + 128] = high
                    tl[i * 128 : i * 128 + 128, j * 128 : j * 128 + 128] = low

    vlane = lax.broadcasted_iota(jnp.int32, (8, 128), 1) & 31
    vtile = jnp.zeros((8, 128), F32)
    for t in range(32):
        vtile = jnp.where(vlane == t, jnp.where(visible[0, t] == 1, 1.0, 0.0), vtile)

    for load in loads:
        load.wait()

    erows_flat = ec.reshape(4 * 1024, 128)

    def erows(half, c):
        return erows_flat[pl.ds(1024 * c + v + 16 * half, 32, stride=32), :]

    for half in range(2):
        for c in range(4):
            epiece[pl.ds(half * 4 + c, 32, stride=8), :] = erows(half, c)
    make_messages(erows, sbox)
    for t in range(16):
        sbox[t, 2] = vtile

    zero = jnp.zeros((32, 512), BF16)
    for ref in (fh, fl, rh, rl):
        ref[0:32, :] = zero
        ref[1504:1536, :] = zero

        @pl.when(b == 0)
        def _():
            for t in range(1, 8):
                ref[t * 32 : t * 32 + 32, :] = zero

        @pl.when(b == 15)
        def _():
            for t in range(40, 47):
                ref[t * 32 : t * 32 + 32, :] = zero

    pl.semaphore_wait(barrier, 30)

    after = b + 1 - 2 * core
    before = b - 1 + 2 * core
    has_after = (after >= 0) & (after < 16)
    has_before = (before >= 0) & (before < 16)
    edge = pltpu.make_async_remote_copy(
        e_hbm.at[pl.ds(25 * (1 - core), 7)], eh.at[core], es, er.at[0], device_id=(v, (after + 16) % 16), device_id_type=MESH
    )

    def exchange(source, target, send, recv, between=None):
        @pl.loop(1, 16)
        def _(d):
            other = (b + d) % 16
            pltpu.make_async_remote_copy(
                source.at[other], target.at[b], send.at[other], recv.at[b],
                device_id=(v, other), device_id_type=MESH,
            ).start()

        if between is not None:
            between()
        target[b] = source[b]

        @pl.loop(1, 16)
        def _(d):
            other = (b + d) % 16
            copy = pltpu.make_async_remote_copy(
                source.at[other], target.at[other], send.at[other], recv.at[other],
                device_id=(v, other), device_id_type=MESH,
            )
            copy.wait_send()
            copy.wait_recv()

    def start_edge():
        @pl.when(has_after)
        def _():
            edge.start()

    exchange(sbox, rbox, a1s, a1r, start_edge)

    take_messages(rbox, piece)
    group = lax.broadcasted_iota(jnp.int32, (8, 128), 1) >> 5
    for c in range(4):
        seen = rbox[4 * c, 2]
        for q in range(1, 4):
            seen = jnp.where(group == q, rbox[4 * c + q, 2], seen)
        visrow[:, 128 * c : 128 * c + 128] = seen

    def gather(own, everything, send, recv, forward, on_piece):
        direct = pltpu.make_async_remote_copy(
            own, everything.at[v], send.at[8], recv.at[v], device_id=(sibling, b), device_id_type=MESH
        )
        for d in (1, 7, 4, 2, 5, 3, 6):
            other = ((chip + d) % 8) * 2 + core
            pltpu.make_async_remote_copy(
                own, everything.at[v], send.at[d], recv.at[v], device_id=(other, b), device_id_type=MESH
            ).start()
        direct.start()
        on_piece(0, own, v)

        @pl.loop(0, 32)
        def _(t):
            rows = pl.ds(pl.multiple_of(t * 8, 8), 8)
            everything.at[v][rows, :] = own[rows, :]

        for d in (1, 7, 4, 2, 5, 3, 6):
            other = ((chip + 8 - d) % 8) * 2 + core
            landed = everything.at[other]
            pltpu.make_async_remote_copy(
                own, landed, send.at[d], recv.at[other], device_id=(other, b), device_id_type=MESH
            ).wait_recv()
            pltpu.make_async_remote_copy(
                landed, landed, forward.at[d], recv.at[other], device_id=(sibling, b), device_id_type=MESH
            ).start()
            on_piece(d, landed, other)

        @pl.loop(0, 8)
        def _(d):
            other = ((chip + 8 - d) % 8) * 2 + 1 - core
            pltpu.make_async_remote_copy(
                own, everything.at[other], send.at[8], recv.at[other], device_id=(sibling, b), device_id_type=MESH
            ).wait_recv()

        direct.wait_send()

        @pl.loop(1, 8)
        def _(d):
            for sem in (send, forward):
                pltpu.make_async_remote_copy(
                    own, everything.at[v], sem.at[d], recv.at[v], device_id=(sibling, b), device_id_type=MESH
                ).wait_send()

    def edge_copy(d, ref, w, slot):
        return pltpu.make_async_remote_copy(
            ref.at[pl.ds(200 * (1 - slot), 56)], tedge.at[w, slot], ts.at[d, slot], tr.at[w, slot],
            device_id=(v, (b + 17 - 2 * slot) % 16), device_id_type=MESH,
        )

    edge_pass = pltpu.make_async_remote_copy(
        eh.at[core], eh.at[core], ef, er.at[1], device_id=(sibling, b), device_id_type=MESH
    )

    def send_edges(d, ref, w):
        if d == 5:

            @pl.when(has_before)
            def _():
                edge.wait_recv()
                edge_pass.start()

        @pl.when(b < 15)
        def _():
            edge_copy(d, ref, w, 0).start()

        @pl.when(b > 0)
        def _():
            edge_copy(d, ref, w, 1).start()

    gather(piece, gathered, g1s, g1r, g1f, send_edges)

    def pass_copy(d, w, slot):
        return pltpu.make_async_remote_copy(
            tedge.at[w, slot], tedge.at[w, slot], tf.at[d, slot], tr.at[w, slot],
            device_id=(sibling, b), device_id_type=MESH,
        )

    flat = gathered.reshape(16 * 256, 128)

    def put(plane, half, c, value):
        rows = pl.ds(pl.multiple_of(plane * 32 + 16 * half, 16), 16)
        high, low = split(value)
        fh[rows, 128 * c : 128 * c + 128] = high
        fl[rows, 128 * c : 128 * c + 128] = low

    @pl.loop(0, 32)
    def _(x):
        for half in range(2):
            for c in range(4):
                swapped = jnp.concatenate(
                    [flat[pl.ds(t * 2048 + x * 8 + half * 4 + c, 8, stride=256), :] for t in range(2)], axis=0
                )
                put(x + 8, half, c, jnp.where(turned, swapped, ec[c, x, 16 * half : 16 * half + 16, :]))

    image_load.wait()
    low_halo = pltpu.make_async_remote_copy(
        redge.at[pl.ds(0, 7)], rhalo.at[1], hs.at[0], hr.at[0],
        device_id=(v, (b + 15) % 16), device_id_type=MESH,
    )
    high_halo = pltpu.make_async_remote_copy(
        redge.at[pl.ds(9, 7)], rhalo.at[0], hs.at[1], hr.at[1],
        device_id=(v, (b + 1) % 16), device_id_type=MESH,
    )

    def ahead(g):
        rows = pl.ds(pl.multiple_of(g * 256, 256), 768)
        high, low = split(dot3(mfh[...], mfl[...], fh[rows, :], fl[rows, :]))
        blurred = dot3(high, low, tfh[...], tfl[...])
        ratio = image[pl.ds(8 * g, 8)].reshape(256, 512) / blurred
        high, low = split(ratio)
        inner = pl.ds(pl.multiple_of(g * 256 + 256, 256), 256)
        rh[inner, :] = high
        rl[inner, :] = low
        return ratio

    ahead(1)

    for slot in range(2):
        here = b > 0 if slot == 0 else b < 15
        there = b < 15 if slot == 0 else b > 0

        @pl.when(here)
        def _():
            for d in (0, 1, 7, 4, 2, 5, 3, 6):
                w = ((chip + 8 - d) % 8) * 2 + core
                edge_copy(d, piece, w, slot).wait_recv()
                pass_copy(d, w, slot).start()

        @pl.when(there)
        def _():
            for d in range(8):
                edge_copy(d, piece, v, slot).wait_send()

    ahead(2)

    edge_flat = tedge.reshape(16 * 112, 128)

    @pl.when(has_before)
    def _():
        edge_pass.wait_send()

    @pl.when(has_after)
    def _():
        edge.wait_send()

    @pl.when(has_after)
    def _():
        pltpu.make_async_remote_copy(
            eh.at[1 - core], eh.at[1 - core], ef, er.at[1], device_id=(sibling, b), device_id_type=MESH
        ).wait_recv()

    for slot in range(2):
        here = b > 0 if slot == 0 else b < 15

        @pl.when(here)
        def _():
            for d in range(8):
                w = ((chip + 8 - d) % 8) * 2 + core
                pass_copy(d, w, slot).wait_send()
                pass_copy(d, ((chip + 8 - d) % 8) * 2 + 1 - core, slot).wait_recv()

            @pl.loop(0, 7)
            def _(x):
                for half in range(2):
                    for c in range(4):
                        start = slot * 56 + x * 8 + half * 4 + c
                        swapped = jnp.concatenate(
                            [edge_flat[pl.ds(t * 896 + start, 8, stride=112), :] for t in range(2)], axis=0
                        )
                        own = eh[slot, x, 16 * half : 16 * half + 16, 128 * c : 128 * c + 128]
                        put(x + 1 + 39 * slot, half, c, jnp.where(turned, swapped, own))

    @pl.loop(0, 2)
    def _(i):
        redge[pl.ds(8 * i, 8)] = ahead(3 * i).reshape(8, 32, 512)

        @pl.when((i == 0) & (b > 0))
        def _():
            low_halo.start()

        @pl.when((i == 1) & (b < 15))
        def _():
            high_halo.start()

    lflat = lp.reshape(16 * PIECE, 128)
    flag = jnp.full((8, 128), jnp.where(turned, 1.0, 0.0), F32)
    for w in range(16):
        lp[w, 0:8, :] = flag

    def back(g, place):
        rows = pl.ds(pl.multiple_of(g * 256, 256), 768)
        high, low = split(dot3(mah[...], mal[...], rh[rows, :], rl[rows, :]))
        correction[...] = dot3(high, low, tah[...], tal[...]).reshape(8, 32, 512)

        @pl.loop(0, 8)
        def _(k):
            seen = jnp.where(visible[0, g * 8 + k] == 1, 1.0, 0.0)
            for c in range(4):
                weight = jnp.where(turned, visrow[:, 128 * c : 128 * c + 128], jnp.full((8, 128), seen, F32))
                for t in range(4):
                    term = weight * jnp.log(correction[k, 8 * t : 8 * t + 8, 128 * c : 128 * c + 128])
                    start = (8 * (t % 2)) * PIECE + (place + k) * 8 + 8 + (t // 2) * 4 + c
                    lflat[pl.ds(start, 8, stride=PIECE), :] = term

    x = chip % 4
    side = chip // 4

    def direct(part, other, origin):
        rows = pl.ds(0, 136) if part == 0 else pl.ds(136, 128)
        return pltpu.make_async_remote_copy(
            lp.at[other, rows], rb.at[origin, rows], rs.at[part, other], rr.at[part, origin],
            device_id=(other, b), device_id_type=MESH,
        )

    def send_part(part):
        for dx, dy, dc in ORDER:
            other = (side + dy - 2 * dy * side) * 8 + ((x + dx) % 4) * 2 + core + dc - 2 * dc * core
            direct(part, other, v).start()

    @pl.loop(0, 2)
    def _(i):
        back(i + 1, 8 * i)

    send_part(0)

    def take_halo(slot):
        @pl.loop(0, 7)
        def _(t):
            high, low = split(rhalo[slot, t])
            rows = pl.ds(pl.multiple_of((t + 1 + 39 * slot) * 32, 32), 32)
            rh[rows, :] = high
            rl[rows, :] = low

    @pl.when(b > 0)
    def _():
        low_halo.wait_send()
        high_halo.wait_recv()
        take_halo(0)

    @pl.when(b < 15)
    def _():
        high_halo.wait_send()
        low_halo.wait_recv()
        take_halo(1)

    @pl.loop(0, 2)
    def _(i):
        back(3 * i, 16 + 8 * i)

    send_part(1)

    def sums(z, place):
        rows = pl.ds(pl.multiple_of(place * 8 + 8, 8), 8)
        up = jnp.zeros((8, 128), F32)
        tp = jnp.zeros((8, 128), F32)
        for w in range(16):
            term = rb[w, rows, :]
            share = term * rb[w, 0:8, :]
            tp = tp + share
            up = up + (term - share)
        rows = pl.ds(pl.multiple_of(z * 8, 8), 8)
        upiece[rows, :] = up
        tpiece[rows, :] = tp

    def take_part(part):
        @pl.loop(0, 17 - part)
        def _(t):
            rows = pl.ds(pl.multiple_of(t * 8 + 136 * part, 8), 8)
            rb.at[v][rows, :] = lp.at[v][rows, :]

        @pl.loop(1, 16)
        def _(d):
            other = (v + d) % 16
            direct(part, other, other).wait_recv()

    take_part(0)

    @pl.loop(0, 16)
    def _(t):
        sums(t + 8, t)

    take_part(1)

    @pl.loop(0, 16)
    def _(t):
        sums(t + 16 * (t // 8), t + 16)

    for part in range(2):
        @pl.loop(1, 16)
        def _(d):
            other = (v + d) % 16
            direct(part, other, other).wait_send()

    make_messages(lambda half, c: tpiece[pl.ds(half * 4 + c, 32, stride=8), :], sbox2)
    exchange(sbox2, rbox2, a2s, a2r)
    take_messages(rbox2, ttpiece)
    upiece[...] = epiece[...] * jnp.exp((upiece[...] + ttpiece[...]) * (1.0 / 16.0))
    gather(upiece, gathered2, g2s, g2r, g2f, lambda d, ref, w: None)

    flat2 = gathered2.reshape(16 * 256, 128)

    @pl.loop(0, 32)
    def _(x):
        for t in range(4):
            for c in range(4):
                start = (8 * (t % 2)) * 256 + x * 8 + (t // 2) * 4 + c
                result[x, 8 * t : 8 * t + 8, 128 * c : 128 * c + 128] = flat2[pl.ds(start, 8, stride=256), :]

    done = pltpu.make_async_copy(result, o_hbm, local_sem.at[0])
    done.start()
    done.wait()


def shards(estimate, image, psf, perm, shift, visible):
    smem = pl.BlockSpec(memory_space=pltpu.SMEM)
    hbm = pl.BlockSpec(memory_space=pl.ANY)
    vmem = pltpu.VMEM
    dma = pltpu.SemaphoreType.DMA
    return pl.pallas_call(
        kernel,
        out_shape=jax.ShapeDtypeStruct(estimate.shape, F32),
        in_specs=[hbm] + [smem] * 3 + [hbm] * 2,
        out_specs=hbm,
        scratch_shapes=[
            pltpu.SMEM((1, 3, 15), F32),
            vmem((4, 32, 32, 128), F32),
            vmem((32, 32, 512), F32),
            vmem((2, 7, 32, 512), F32),
            vmem((16, 2, 56, 128), F32),
        ]
        + [vmem((1536, 512), BF16)] * 4
        + [vmem((16, 32, 512), F32), vmem((2, 7, 32, 512), F32)]
        + [vmem((256, 768), BF16)] * 4
        + [vmem((512, 512), BF16)] * 4
        + [
            vmem((16, 3, 8, 128), F32),
            vmem((16, 3, 8, 128), F32),
            vmem((16, 2, 8, 128), F32),
            vmem((16, 2, 8, 128), F32),
            vmem((8, 512), F32),
            vmem((256, 128), F32),
            vmem((256, 128), F32),
            vmem((16, 256, 128), F32),
            vmem((8, 32, 512), F32),
            vmem((16, PIECE, 128), F32),
            vmem((16, PIECE, 128), F32),
            vmem((256, 128), F32),
            vmem((256, 128), F32),
            vmem((256, 128), F32),
            vmem((16, 256, 128), F32),
            vmem((32, 32, 512), F32),
            dma((6,)),
        ]
        + [dma((16,))] * 4
        + [dma((9,)), dma((16,)), dma((8,))] * 2
        + [dma, dma((2,)), dma]
        + [dma((8, 2)), dma((16, 2)), dma((8, 2))]
        + [dma((2,)), dma((2,)), dma((2, 16)), dma((2, 16))],
        compiler_params=pltpu.CompilerParams(
            collective_id=0, has_side_effects=True, vmem_limit_bytes=60 * 1024 * 1024
        ),
    )(psf, perm, shift, visible, estimate, image)


def solution(mesh):
    placed = (
        P("bulk", None, None),
        P("view", "bulk", None, None),
        P("view", None, None),
        P("view"),
        P("view"),
        P("view", "bulk"),
    )
    return jax.shard_map(
        shards, mesh=mesh, in_specs=placed, out_specs=P("bulk", None, None), check_vma=False
    )
```

```python
import jax
import jax.numpy as jnp
from jax import lax
from jax.experimental import pallas as pl
from jax.experimental.pallas import tpu as pltpu
from jax.sharding import PartitionSpec as P

MESH = pl.DeviceIdType.MESH
F32 = jnp.float32
BF16 = jnp.bfloat16
PIECE = 33 * 8


def split(x):
    high = x.astype(BF16)
    return high, (x - high.astype(F32)).astype(BF16)


def dot3(ah, al, bh, bl):
    def dot(a, b):
        return lax.dot_general(a, b, (((1,), (0,)), ((), ())), preferred_element_type=F32)

    return dot(ah, bh) + dot(ah, bl) + dot(al, bh)


def lane_groups(ins):
    group = lax.broadcasted_iota(jnp.int32, (8, 128), 1) >> 5
    outs = []
    for i in range(4):
        out = ins[i]
        for j in range(4):
            if j != i:
                out = jnp.where(group == j, pltpu.roll(ins[j], (32 * (j - i)) % 128, 1), out)
        outs.append(out)
    return outs


def make_messages(load, box):
    for half in range(2):
        stacked = jnp.concatenate([load(half, c) for c in range(4)], axis=0)
        turned = stacked.T
        for r in range(4):
            outs = lane_groups([turned[r * 32 + q * 8 : r * 32 + q * 8 + 8] for q in range(4)])
            for c in range(4):
                box[4 * c + r, half] = outs[c]


def take_messages(box, piece):
    for half in range(2):
        for c in range(4):
            outs = lane_groups([box[4 * c + r, half] for r in range(4)])
            for q in range(4):
                piece[pl.ds(q * 64 + half * 4 + c, 8, stride=8), :] = outs[q]


ORDER = (
    (1, 0, 0), (3, 0, 0), (0, 1, 0), (1, 0, 1), (3, 0, 1), (0, 1, 1), (2, 0, 0), (1, 1, 0),
    (3, 1, 0), (2, 0, 1), (1, 1, 1), (3, 1, 1), (2, 1, 0), (2, 1, 1), (0, 0, 1),
)


def kernel(
    psf_hbm, perm, shift, visible, e_hbm, i_hbm, o_hbm,
    psf, ec, image, eh, tedge, fh, fl, rh, rl, redge, rhalo, mfh, mfl, mah, mal, tfh, tfl, tah, tal,
    sbox, rbox, sbox2, rbox2, visrow, epiece, piece, gathered, correction, lp, rb,
    upiece, tpiece, ttpiece, gathered2,
    local_sem, os, a1s, a1r, a2s, a2r, g1s, g1r, g1f, g2s, g2r, g2f, es, er, ef, ts, tr, tf, hs, hr, rs, rr,
):
    v = lax.axis_index("view")
    b = lax.axis_index("bulk")
    core = v % 2
    chip = v // 2
    sibling = v + 1 - 2 * core

    psf_load = pltpu.make_async_copy(psf_hbm, psf, local_sem.at[5])
    psf_load.start()
    loads = [
        pltpu.make_async_copy(e_hbm.at[:, :, pl.ds(128 * c, 128)], ec.at[c], local_sem.at[c])
        for c in range(4)
    ]
    image_load = pltpu.make_async_copy(i_hbm.at[0], image, local_sem.at[4])
    for load in loads:
        load.start()
    image_load.start()

    barrier = pltpu.get_barrier_semaphore()

    @pl.loop(1, 16)
    def _(d):
        pl.semaphore_signal(barrier, inc=1, device_id=((v + d) % 16, b), device_id_type=MESH)
        pl.semaphore_signal(barrier, inc=1, device_id=(v, (b + d) % 16), device_id_type=MESH)

    turned = perm[0] == 1
    moved = shift[0]

    vlane = lax.broadcasted_iota(jnp.int32, (8, 128), 1) & 31
    vtile = jnp.zeros((8, 128), F32)
    for t in range(32):
        vtile = jnp.where(vlane == t, jnp.where(visible[0, t] == 1, 1.0, 0.0), vtile)

    for load in loads:
        load.wait()

    erows_flat = ec.reshape(4 * 1024, 128)

    def erows(half, c):
        return erows_flat[pl.ds(1024 * c + v + 16 * half, 32, stride=32), :]

    for half in range(2):
        for c in range(4):
            epiece[pl.ds(half * 4 + c, 32, stride=8), :] = erows(half, c)
    make_messages(erows, sbox)
    for t in range(16):
        sbox[t, 2] = vtile

    pl.semaphore_wait(barrier, 30)

    after = b + 1 - 2 * core
    before = b - 1 + 2 * core
    has_after = (after >= 0) & (after < 16)
    has_before = (before >= 0) & (before < 16)
    edge = pltpu.make_async_remote_copy(
        e_hbm.at[pl.ds(25 * (1 - core), 7)], eh.at[core], es, er.at[0], device_id=(v, (after + 16) % 16), device_id_type=MESH
    )

    def exchange(source, target, send, recv, between=None):
        @pl.loop(1, 16)
        def _(d):
            other = (b + d) % 16
            pltpu.make_async_remote_copy(
                source.at[other], target.at[b], send.at[other], recv.at[b],
                device_id=(v, other), device_id_type=MESH,
            ).start()

        if between is not None:
            between()
        target[b] = source[b]

        @pl.loop(1, 16)
        def _(d):
            other = (b + d) % 16
            copy = pltpu.make_async_remote_copy(
                source.at[other], target.at[other], send.at[other], recv.at[other],
                device_id=(v, other), device_id_type=MESH,
            )
            copy.wait_send()
            copy.wait_recv()

    def start_edge():
        @pl.when(has_after)
        def _():
            edge.start()

        psf_load.wait()

        row = lax.broadcasted_iota(jnp.int32, (32, 128), 0)
        lane = lax.broadcasted_iota(jnp.int32, (32, 128), 1)

        def pick(index, axis, reverse, shape):
            total = psf[axis, 0, 0]
            for t in range(1, 15):
                total = total + psf[axis, 0, t]
            out = jnp.zeros(shape, F32)
            for t in range(15):
                out = jnp.where(index == t, psf[axis, 0, 14 - t if reverse else t], out)
            return out / jnp.full(shape, total, F32)

        zlane = lax.broadcasted_iota(jnp.int32, (8, 768), 1) >> 5
        brow = lax.broadcasted_iota(jnp.int32, (128, 128), 0)
        blane = lax.broadcasted_iota(jnp.int32, (128, 128), 1)
        for reverse, mh, ml, th, tl in ((False, mfh, mfl, tfh, tfl), (True, mah, mal, tah, tal)):
            offset = -moved if reverse else moved
            circ = pick(((lane & 31) - row + 7 + offset) & 31, 1, reverse, (32, 128))
            wide = jnp.concatenate([circ] * 6, axis=1)
            for zo in range(8):
                zrow = pick(zlane - zo - 1, 0, reverse, (8, 768))
                high, low = split(wide * zrow[0:1])
                mh[zo * 32 : zo * 32 + 32, :] = high
                ml[zo * 32 : zo * 32 + 32, :] = low
            th[...] = jnp.zeros((512, 512), BF16)
            tl[...] = jnp.zeros((512, 512), BF16)
            for delta in (-1, 0, 1):
                high, low = split(pick(brow - blane - 128 * delta + 7, 2, reverse, (128, 128)))
                for i in range(4):
                    j = i + delta
                    if 0 <= j < 4:
                        th[i * 128 : i * 128 + 128, j * 128 : j * 128 + 128] = high
                        tl[i * 128 : i * 128 + 128, j * 128 : j * 128 + 128] = low

        zero = jnp.zeros((32, 512), BF16)
        for ref in (fh, fl, rh, rl):
            ref[0:32, :] = zero
            ref[1504:1536, :] = zero

            @pl.when(b == 0)
            def _():
                for t in range(1, 8):
                    ref[t * 32 : t * 32 + 32, :] = zero

            @pl.when(b == 15)
            def _():
                for t in range(40, 47):
                    ref[t * 32 : t * 32 + 32, :] = zero

    exchange(sbox, rbox, a1s, a1r, start_edge)

    take_messages(rbox, piece)
    group = lax.broadcasted_iota(jnp.int32, (8, 128), 1) >> 5
    for c in range(4):
        seen = rbox[4 * c, 2]
        for q in range(1, 4):
            seen = jnp.where(group == q, rbox[4 * c + q, 2], seen)
        visrow[:, 128 * c : 128 * c + 128] = seen

    def gather(own, everything, send, recv, forward, on_piece, on_passed=None):
        direct = pltpu.make_async_remote_copy(
            own, everything.at[v], send.at[8], recv.at[v], device_id=(sibling, b), device_id_type=MESH
        )
        for d in (1, 7, 4, 2, 5, 3, 6):
            other = ((chip + d) % 8) * 2 + core
            pltpu.make_async_remote_copy(
                own, everything.at[v], send.at[d], recv.at[v], device_id=(other, b), device_id_type=MESH
            ).start()
        direct.start()
        on_piece(0, own, v)

        @pl.loop(0, 32)
        def _(t):
            rows = pl.ds(pl.multiple_of(t * 8, 8), 8)
            everything.at[v][rows, :] = own[rows, :]

        for d in (1, 7, 4, 2, 5, 3, 6):
            other = ((chip + 8 - d) % 8) * 2 + core
            landed = everything.at[other]
            pltpu.make_async_remote_copy(
                own, landed, send.at[d], recv.at[other], device_id=(other, b), device_id_type=MESH
            ).wait_recv()
            pltpu.make_async_remote_copy(
                landed, landed, forward.at[d], recv.at[other], device_id=(sibling, b), device_id_type=MESH
            ).start()
            on_piece(d, landed, other)

        @pl.loop(0, 8)
        def _(d):
            other = ((chip + 8 - d) % 8) * 2 + 1 - core
            pltpu.make_async_remote_copy(
                own, everything.at[other], send.at[8], recv.at[other], device_id=(sibling, b), device_id_type=MESH
            ).wait_recv()
            if on_passed is not None:
                on_passed(everything.at[other], other).start()

        direct.wait_send()

        @pl.loop(1, 8)
        def _(d):
            for sem in (send, forward):
                pltpu.make_async_remote_copy(
                    own, everything.at[v], sem.at[d], recv.at[v], device_id=(sibling, b), device_id_type=MESH
                ).wait_send()

    def edge_copy(d, ref, w, slot):
        return pltpu.make_async_remote_copy(
            ref.at[pl.ds(200 * (1 - slot), 56)], tedge.at[w, slot], ts.at[d, slot], tr.at[w, slot],
            device_id=(v, (b + 17 - 2 * slot) % 16), device_id_type=MESH,
        )

    edge_pass = pltpu.make_async_remote_copy(
        eh.at[core], eh.at[core], ef, er.at[1], device_id=(sibling, b), device_id_type=MESH
    )

    def send_edges(d, ref, w):
        if d == 5:

            @pl.when(has_before)
            def _():
                edge.wait_recv()
                edge_pass.start()

        @pl.when(b < 15)
        def _():
            edge_copy(d, ref, w, 0).start()

        @pl.when(b > 0)
        def _():
            edge_copy(d, ref, w, 1).start()

    gather(piece, gathered, g1s, g1r, g1f, send_edges)

    def pass_copy(d, w, slot):
        return pltpu.make_async_remote_copy(
            tedge.at[w, slot], tedge.at[w, slot], tf.at[d, slot], tr.at[w, slot],
            device_id=(sibling, b), device_id_type=MESH,
        )

    flat = gathered.reshape(16 * 256, 128)

    def put(plane, half, c, value):
        rows = pl.ds(pl.multiple_of(plane * 32 + 16 * half, 16), 16)
        high, low = split(value)
        fh[rows, 128 * c : 128 * c + 128] = high
        fl[rows, 128 * c : 128 * c + 128] = low

    @pl.loop(0, 32)
    def _(x):
        for half in range(2):
            for c in range(4):
                swapped = jnp.concatenate(
                    [flat[pl.ds(t * 2048 + x * 8 + half * 4 + c, 8, stride=256), :] for t in range(2)], axis=0
                )
                put(x + 8, half, c, jnp.where(turned, swapped, ec[c, x, 16 * half : 16 * half + 16, :]))

    image_load.wait()
    low_halo = pltpu.make_async_remote_copy(
        redge.at[pl.ds(0, 7)], rhalo.at[1], hs.at[0], hr.at[0],
        device_id=(v, (b + 15) % 16), device_id_type=MESH,
    )
    high_halo = pltpu.make_async_remote_copy(
        redge.at[pl.ds(9, 7)], rhalo.at[0], hs.at[1], hr.at[1],
        device_id=(v, (b + 1) % 16), device_id_type=MESH,
    )

    def ahead(g):
        rows = pl.ds(pl.multiple_of(g * 256, 256), 768)
        high, low = split(dot3(mfh[...], mfl[...], fh[rows, :], fl[rows, :]))
        blurred = dot3(high, low, tfh[...], tfl[...])
        ratio = image[pl.ds(8 * g, 8)].reshape(256, 512) / blurred
        high, low = split(ratio)
        inner = pl.ds(pl.multiple_of(g * 256 + 256, 256), 256)
        rh[inner, :] = high
        rl[inner, :] = low
        return ratio

    ahead(1)

    for slot in range(2):
        here = b > 0 if slot == 0 else b < 15
        there = b < 15 if slot == 0 else b > 0

        @pl.when(here)
        def _():
            for d in (0, 1, 7, 4, 2, 5, 3, 6):
                w = ((chip + 8 - d) % 8) * 2 + core
                edge_copy(d, piece, w, slot).wait_recv()
                pass_copy(d, w, slot).start()

        @pl.when(there)
        def _():
            for d in range(8):
                edge_copy(d, piece, v, slot).wait_send()

    ahead(2)

    edge_flat = tedge.reshape(16 * 112, 128)

    @pl.when(has_before)
    def _():
        edge_pass.wait_send()

    @pl.when(has_after)
    def _():
        edge.wait_send()

    @pl.when(has_after)
    def _():
        pltpu.make_async_remote_copy(
            eh.at[1 - core], eh.at[1 - core], ef, er.at[1], device_id=(sibling, b), device_id_type=MESH
        ).wait_recv()

    for slot in range(2):
        here = b > 0 if slot == 0 else b < 15

        @pl.when(here)
        def _():
            for d in range(8):
                w = ((chip + 8 - d) % 8) * 2 + core
                pass_copy(d, w, slot).wait_send()
                pass_copy(d, ((chip + 8 - d) % 8) * 2 + 1 - core, slot).wait_recv()

            @pl.loop(0, 7)
            def _(x):
                for half in range(2):
                    for c in range(4):
                        start = slot * 56 + x * 8 + half * 4 + c
                        swapped = jnp.concatenate(
                            [edge_flat[pl.ds(t * 896 + start, 8, stride=112), :] for t in range(2)], axis=0
                        )
                        own = eh[slot, x, 16 * half : 16 * half + 16, 128 * c : 128 * c + 128]
                        put(x + 1 + 39 * slot, half, c, jnp.where(turned, swapped, own))

    @pl.loop(0, 2)
    def _(i):
        redge[pl.ds(8 * i, 8)] = ahead(3 * i).reshape(8, 32, 512)

        @pl.when((i == 0) & (b > 0))
        def _():
            low_halo.start()

        @pl.when((i == 1) & (b < 15))
        def _():
            high_halo.start()

    lflat = lp.reshape(16 * PIECE, 128)
    flag = jnp.full((8, 128), jnp.where(turned, 1.0, 0.0), F32)
    for w in range(16):
        lp[w, 0:8, :] = flag

    def back(g, place):
        rows = pl.ds(pl.multiple_of(g * 256, 256), 768)
        high, low = split(dot3(mah[...], mal[...], rh[rows, :], rl[rows, :]))
        correction[...] = dot3(high, low, tah[...], tal[...]).reshape(8, 32, 512)

        @pl.loop(0, 8)
        def _(k):
            seen = jnp.where(visible[0, g * 8 + k] == 1, 1.0, 0.0)
            for c in range(4):
                weight = jnp.where(turned, visrow[:, 128 * c : 128 * c + 128], jnp.full((8, 128), seen, F32))
                for t in range(4):
                    term = weight * jnp.log(correction[k, 8 * t : 8 * t + 8, 128 * c : 128 * c + 128])
                    start = (8 * (t % 2)) * PIECE + (place + k) * 8 + 8 + (t // 2) * 4 + c
                    lflat[pl.ds(start, 8, stride=PIECE), :] = term

    x = chip % 4
    side = chip // 4

    def direct(part, other, origin):
        rows = pl.ds(0, 136) if part == 0 else pl.ds(136, 128)
        return pltpu.make_async_remote_copy(
            lp.at[other, rows], rb.at[origin, rows], rs.at[part, other], rr.at[part, origin],
            device_id=(other, b), device_id_type=MESH,
        )

    def send_part(part):
        for which, order in ((0, [(1, 0, 0), (3, 0, 0), (0, 1, 0), (1, 0, 1), (3, 0, 1), (0, 1, 1), (2, 0, 0), (1, 1, 0), (3, 1, 0), (2, 0, 1), (1, 1, 1), (3, 1, 1), (2, 1, 0), (2, 1, 1), (0, 0, 1)]), (1, [(1, 1, 0), (3, 1, 0), (0, 1, 0), (2, 1, 0), (1, 1, 1), (3, 1, 1), (0, 1, 1), (2, 1, 1), (1, 0, 0), (3, 0, 0), (2, 0, 0), (1, 0, 1), (3, 0, 1), (2, 0, 1), (0, 0, 1)])):
            @pl.when(core == which)
            def _():
                for dx, dy, dc in order:
                    other = (side + dy - 2 * dy * side) * 8 + ((x + dx) % 4) * 2 + core + dc - 2 * dc * core
                    direct(part, other, v).start()

    @pl.loop(0, 2)
    def _(i):
        back(i + 1, 8 * i)

    send_part(0)

    def take_halo(slot):
        @pl.loop(0, 7)
        def _(t):
            high, low = split(rhalo[slot, t])
            rows = pl.ds(pl.multiple_of((t + 1 + 39 * slot) * 32, 32), 32)
            rh[rows, :] = high
            rl[rows, :] = low

    @pl.when(b > 0)
    def _():
        low_halo.wait_send()
        high_halo.wait_recv()
        take_halo(0)

    @pl.when(b < 15)
    def _():
        high_halo.wait_send()
        low_halo.wait_recv()
        take_halo(1)

    @pl.loop(0, 2)
    def _(i):
        back(3 * i, 16 + 8 * i)

    send_part(1)

    def sums(z, place):
        rows = pl.ds(pl.multiple_of(place * 8 + 8, 8), 8)
        up = jnp.zeros((8, 128), F32)
        tp = jnp.zeros((8, 128), F32)
        for w in range(16):
            term = rb[w, rows, :]
            share = term * rb[w, 0:8, :]
            tp = tp + share
            up = up + (term - share)
        rows = pl.ds(pl.multiple_of(z * 8, 8), 8)
        upiece[rows, :] = up
        tpiece[rows, :] = tp

    def take_part(part):
        @pl.loop(0, 17 - part)
        def _(t):
            rows = pl.ds(pl.multiple_of(t * 8 + 136 * part, 8), 8)
            rb.at[v][rows, :] = lp.at[v][rows, :]

        @pl.loop(1, 16)
        def _(d):
            other = (v + d) % 16
            direct(part, other, other).wait_recv()

    take_part(0)

    @pl.loop(0, 16)
    def _(t):
        sums(t + 8, t)

    take_part(1)

    @pl.loop(0, 16)
    def _(t):
        sums(t + 16 * (t // 8), t + 16)

    for part in range(2):
        @pl.loop(1, 16)
        def _(d):
            other = (v + d) % 16
            direct(part, other, other).wait_send()

    make_messages(lambda half, c: tpiece[pl.ds(half * 4 + c, 32, stride=8), :], sbox2)
    exchange(sbox2, rbox2, a2s, a2r)
    take_messages(rbox2, ttpiece)
    upiece[...] = epiece[...] * jnp.exp((upiece[...] + ttpiece[...]) * (1.0 / 16.0))

    def out_copy(ref, w):
        return pltpu.make_async_copy(ref, o_hbm.at[w], os.at[w])

    gather(upiece, gathered2, g2s, g2r, g2f, lambda d, ref, w: out_copy(ref, w).start(), out_copy)

    @pl.loop(0, 16)
    def _(w):
        out_copy(upiece, w).wait()


def reorder(pieces, out):
    flat = pieces.reshape(16 * 128, 128)

    @pl.loop(0, 16)
    def _(x):
        for t in range(4):
            for c in range(4):
                start = (8 * (t % 2)) * 128 + x * 8 + (t // 2) * 4 + c
                out[x, 8 * t : 8 * t + 8, 128 * c : 128 * c + 128] = flat[pl.ds(start, 8, stride=128), :]


def shards(estimate, image, psf, perm, shift, visible):
    smem = pl.BlockSpec(memory_space=pltpu.SMEM)
    hbm = pl.BlockSpec(memory_space=pl.ANY)
    vmem = pltpu.VMEM
    dma = pltpu.SemaphoreType.DMA
    pieces = pl.pallas_call(
        kernel,
        out_shape=jax.ShapeDtypeStruct((16, 256, 128), F32),
        in_specs=[hbm] + [smem] * 3 + [hbm] * 2,
        out_specs=hbm,
        scratch_shapes=[
            pltpu.SMEM((3, 1, 15), F32),
            vmem((4, 32, 32, 128), F32),
            vmem((32, 32, 512), F32),
            vmem((2, 7, 32, 512), F32),
            vmem((16, 2, 56, 128), F32),
        ]
        + [vmem((1536, 512), BF16)] * 4
        + [vmem((16, 32, 512), F32), vmem((2, 7, 32, 512), F32)]
        + [vmem((256, 768), BF16)] * 4
        + [vmem((512, 512), BF16)] * 4
        + [
            vmem((16, 3, 8, 128), F32),
            vmem((16, 3, 8, 128), F32),
            vmem((16, 2, 8, 128), F32),
            vmem((16, 2, 8, 128), F32),
            vmem((8, 512), F32),
            vmem((256, 128), F32),
            vmem((256, 128), F32),
            vmem((16, 256, 128), F32),
            vmem((8, 32, 512), F32),
            vmem((16, PIECE, 128), F32),
            vmem((16, PIECE, 128), F32),
            vmem((256, 128), F32),
            vmem((256, 128), F32),
            vmem((256, 128), F32),
            vmem((16, 256, 128), F32),
            dma((6,)),
            dma((16,)),
        ]
        + [dma((16,))] * 4
        + [dma((9,)), dma((16,)), dma((8,))] * 2
        + [dma, dma((2,)), dma]
        + [dma((8, 2)), dma((16, 2)), dma((8, 2))]
        + [dma((2,)), dma((2,)), dma((2, 16)), dma((2, 16))],
        compiler_params=pltpu.CompilerParams(
            collective_id=0, has_side_effects=True, vmem_limit_bytes=60 * 1024 * 1024
        ),
    )(jnp.transpose(psf, (1, 0, 2)), perm, shift, visible, estimate, image)
    return pl.pallas_call(
        reorder,
        out_shape=jax.ShapeDtypeStruct(estimate.shape, F32),
        grid=(2,),
        in_specs=[pl.BlockSpec((16, 128, 128), lambda i: (0, i, 0))],
        out_specs=pl.BlockSpec((16, 32, 512), lambda i: (i, 0, 0)),
    )(pieces)


def solution(mesh):
    placed = (
        P("bulk", None, None),
        P("view", "bulk", None, None),
        P("view", None, None),
        P("view"),
        P("view"),
        P("view", "bulk"),
    )
    return jax.shard_map(
        shards, mesh=mesh, in_specs=placed, out_specs=P("bulk", None, None), check_vma=False
    )
```

```python
import jax
import jax.numpy as jnp
from jax import lax
from jax.experimental import pallas as pl
from jax.experimental.pallas import tpu as pltpu
from jax.sharding import PartitionSpec as P

MESH = pl.DeviceIdType.MESH
F32 = jnp.float32
BF16 = jnp.bfloat16
PIECE = 33 * 8


def split(x):
    high = x.astype(BF16)
    return high, (x - high.astype(F32)).astype(BF16)


def dot3(ah, al, bh, bl):
    def dot(a, b):
        return lax.dot_general(a, b, (((1,), (0,)), ((), ())), preferred_element_type=F32)

    return dot(ah, bh) + dot(ah, bl) + dot(al, bh)


def lane_groups(ins):
    group = lax.broadcasted_iota(jnp.int32, (8, 128), 1) >> 5
    outs = []
    for i in range(4):
        out = ins[i]
        for j in range(4):
            if j != i:
                out = jnp.where(group == j, pltpu.roll(ins[j], (32 * (j - i)) % 128, 1), out)
        outs.append(out)
    return outs


def make_messages(load, box):
    for half in range(2):
        stacked = jnp.concatenate([load(half, c) for c in range(4)], axis=0)
        turned = stacked.T
        for r in range(4):
            outs = lane_groups([turned[r * 32 + q * 8 : r * 32 + q * 8 + 8] for q in range(4)])
            for c in range(4):
                box[4 * c + r, half] = outs[c]


def take_messages(box, piece):
    for half in range(2):
        for c in range(4):
            outs = lane_groups([box[4 * c + r, half] for r in range(4)])
            for q in range(4):
                piece[pl.ds(q * 64 + half * 4 + c, 8, stride=8), :] = outs[q]


ORDER = (
    (1, 0, 0), (3, 0, 0), (0, 1, 0), (1, 0, 1), (3, 0, 1), (0, 1, 1), (2, 0, 0), (1, 1, 0),
    (3, 1, 0), (2, 0, 1), (1, 1, 1), (3, 1, 1), (2, 1, 0), (2, 1, 1), (0, 0, 1),
)


def kernel(
    psf_hbm, perm, shift, visible, e_hbm, i_hbm, o_hbm,
    psf, ec, image, eh, tedge, fh, fl, rh, rl, redge, rhalo, mfh, mfl, mah, mal, tfh, tfl, tah, tal,
    sbox, rbox, sbox2, rbox2, visrow, epiece, piece, gathered, correction, lp, rb,
    upiece, tpiece, ttpiece, gathered2,
    local_sem, os, a1s, a1r, a2s, a2r, g1s, g1r, g2s, g2r, es, er, ef, ts, tr, tf, hs, hr, rs, rr,
):
    v = lax.axis_index("view")
    b = lax.axis_index("bulk")
    core = v % 2
    chip = v // 2
    sibling = v + 1 - 2 * core
    column = chip % 4
    side = chip // 4

    def view_at(dx, dy, dc=0):
        return (side + dy - 2 * dy * side) * 8 + ((column + dx) % 4) * 2 + core + dc - 2 * dc * core


    psf_load = pltpu.make_async_copy(psf_hbm, psf, local_sem.at[5])
    psf_load.start()
    loads = [
        pltpu.make_async_copy(e_hbm.at[:, :, pl.ds(128 * c, 128)], ec.at[c], local_sem.at[c])
        for c in range(4)
    ]
    image_load = pltpu.make_async_copy(i_hbm.at[0], image, local_sem.at[4])
    for load in loads:
        load.start()
    image_load.start()

    barrier = pltpu.get_barrier_semaphore()

    @pl.loop(1, 16)
    def _(d):
        pl.semaphore_signal(barrier, inc=1, device_id=((v + d) % 16, b), device_id_type=MESH)
        pl.semaphore_signal(barrier, inc=1, device_id=(v, (b + d) % 16), device_id_type=MESH)

    turned = perm[0] == 1
    moved = shift[0]

    vlane = lax.broadcasted_iota(jnp.int32, (8, 128), 1) & 31
    vtile = jnp.zeros((8, 128), F32)
    for t in range(32):
        vtile = jnp.where(vlane == t, jnp.where(visible[0, t] == 1, 1.0, 0.0), vtile)

    for load in loads:
        load.wait()

    erows_flat = ec.reshape(4 * 1024, 128)

    def erows(half, c):
        return erows_flat[pl.ds(1024 * c + v + 16 * half, 32, stride=32), :]

    for half in range(2):
        for c in range(4):
            epiece[pl.ds(half * 4 + c, 32, stride=8), :] = erows(half, c)
    make_messages(erows, sbox)
    for t in range(16):
        sbox[t, 2] = vtile

    pl.semaphore_wait(barrier, 30)

    after = b + 1 - 2 * core
    before = b - 1 + 2 * core
    has_after = (after >= 0) & (after < 16)
    has_before = (before >= 0) & (before < 16)
    edge = pltpu.make_async_remote_copy(
        e_hbm.at[pl.ds(25 * (1 - core), 7)], eh.at[core], es, er.at[0], device_id=(v, (after + 16) % 16), device_id_type=MESH
    )

    def exchange(source, target, send, recv, between=None):
        @pl.loop(1, 16)
        def _(d):
            other = (b + d) % 16
            pltpu.make_async_remote_copy(
                source.at[other], target.at[b], send.at[other], recv.at[b],
                device_id=(v, other), device_id_type=MESH,
            ).start()

        if between is not None:
            between()
        target[b] = source[b]

        @pl.loop(1, 16)
        def _(d):
            other = (b + d) % 16
            copy = pltpu.make_async_remote_copy(
                source.at[other], target.at[other], send.at[other], recv.at[other],
                device_id=(v, other), device_id_type=MESH,
            )
            copy.wait_send()
            copy.wait_recv()

    def start_edge():
        @pl.when(has_after)
        def _():
            edge.start()

        psf_load.wait()

        row = lax.broadcasted_iota(jnp.int32, (32, 128), 0)
        lane = lax.broadcasted_iota(jnp.int32, (32, 128), 1)

        def pick(index, axis, reverse, shape):
            total = psf[axis, 0, 0]
            for t in range(1, 15):
                total = total + psf[axis, 0, t]
            out = jnp.zeros(shape, F32)
            for t in range(15):
                out = jnp.where(index == t, psf[axis, 0, 14 - t if reverse else t], out)
            return out / jnp.full(shape, total, F32)

        zlane = lax.broadcasted_iota(jnp.int32, (8, 768), 1) >> 5
        brow = lax.broadcasted_iota(jnp.int32, (128, 128), 0)
        blane = lax.broadcasted_iota(jnp.int32, (128, 128), 1)
        for reverse, mh, ml, th, tl in ((False, mfh, mfl, tfh, tfl), (True, mah, mal, tah, tal)):
            offset = -moved if reverse else moved
            circ = pick(((lane & 31) - row + 7 + offset) & 31, 1, reverse, (32, 128))
            wide = jnp.concatenate([circ] * 6, axis=1)
            for zo in range(8):
                zrow = pick(zlane - zo - 1, 0, reverse, (8, 768))
                high, low = split(wide * zrow[0:1])
                mh[zo * 32 : zo * 32 + 32, :] = high
                ml[zo * 32 : zo * 32 + 32, :] = low
            th[...] = jnp.zeros((512, 512), BF16)
            tl[...] = jnp.zeros((512, 512), BF16)
            for delta in (-1, 0, 1):
                high, low = split(pick(brow - blane - 128 * delta + 7, 2, reverse, (128, 128)))
                for i in range(4):
                    j = i + delta
                    if 0 <= j < 4:
                        th[i * 128 : i * 128 + 128, j * 128 : j * 128 + 128] = high
                        tl[i * 128 : i * 128 + 128, j * 128 : j * 128 + 128] = low

        zero = jnp.zeros((32, 512), BF16)
        for ref in (fh, fl, rh, rl):
            ref[0:32, :] = zero
            ref[1504:1536, :] = zero

            @pl.when(b == 0)
            def _():
                for t in range(1, 8):
                    ref[t * 32 : t * 32 + 32, :] = zero

            @pl.when(b == 15)
            def _():
                for t in range(40, 47):
                    ref[t * 32 : t * 32 + 32, :] = zero

    exchange(sbox, rbox, a1s, a1r, start_edge)

    take_messages(rbox, piece)
    group = lax.broadcasted_iota(jnp.int32, (8, 128), 1) >> 5
    for c in range(4):
        seen = rbox[4 * c, 2]
        for q in range(1, 4):
            seen = jnp.where(group == q, rbox[4 * c + q, 2], seen)
        visrow[:, 128 * c : 128 * c + 128] = seen

    def gather(own, everything, send, recv, on_half, on_passed):
        used = []

        def place(h):
            return (h + core) % 2

        def rows(h):
            return pl.ds(pl.multiple_of(128 * place(h), 128), 128)

        def push(w, h, target, source=None):
            copy = pltpu.make_async_remote_copy(
                (everything.at[w] if source is None else source).at[rows(h)], everything.at[w, rows(h)],
                send.at[len(used)], recv.at[w, place(h)], device_id=(target, b), device_id_type=MESH,
            )
            copy.start()
            used.append(copy)

        def landed(w, h):
            pltpu.make_async_remote_copy(
                own.at[rows(h)], everything.at[w, rows(h)], send.at[0], recv.at[w, place(h)],
                device_id=(sibling, b), device_id_type=MESH,
            ).wait_recv()

        right, left, across, far = view_at(1, 0), view_at(3, 0), view_at(0, 1), view_at(2, 0)
        for first, second in ((across, right), (right, left), (left, far), (far, across)):
            push(v, 0, first, own)
            push(v, 1, second, own)
        for h in range(2):
            push(v, h, sibling, own)
            on_half(0, own, v, rows(h), place(h))

        @pl.loop(0, 32)
        def _(t):
            tile = pl.ds(pl.multiple_of(t * 8, 8), 8)
            everything.at[v][tile, :] = own[tile, :]

        def relay(dx, dy, h, targets):
            w = view_at(dx, dy)
            landed(w, h)
            for target in targets:
                push(w, h, target)
            push(w, h, sibling)
            on_half(dx + 4 * dy, everything.at[w], w, rows(h), place(h))

        relay(0, 1, 0, (right, left, far))
        relay(3, 0, 1, (across,))
        relay(1, 0, 1, (across,))
        relay(3, 0, 0, ())
        relay(1, 0, 0, ())
        relay(2, 0, 1, (across,))
        relay(2, 0, 0, ())
        relay(0, 1, 1, ())
        for dx in (3, 1, 2):
            for h in range(2):
                relay(dx, 1, h, ())

        for dy in range(2):
            for dx in range(4):
                w = view_at(dx, dy, 1)
                for h in range(2):
                    landed(w, h)
                    on_passed(everything.at[w], w, rows(h), place(h))

        for copy in used:
            copy.wait_send()

    def edge_copy(d, ref, w, slot):
        return pltpu.make_async_remote_copy(
            ref.at[pl.ds(200 * (1 - slot), 56)], tedge.at[w, slot], ts.at[d, slot], tr.at[w, slot],
            device_id=(v, (b + 17 - 2 * slot) % 16), device_id_type=MESH,
        )

    edge_pass = pltpu.make_async_remote_copy(
        eh.at[core], eh.at[core], ef, er.at[1], device_id=(sibling, b), device_id_type=MESH
    )

    halves = []

    def send_edges(d, ref, w, rows, half):
        target = b - 1 + 2 * half

        @pl.when((target >= 0) & (target < 16))
        def _():
            edge_copy(d, ref, w, 1 - half).start()

        halves.append(d)
        if len(halves) == 8:

            @pl.when(has_before)
            def _():
                edge.wait_recv()
                edge_pass.start()

    gather(piece, gathered, g1s, g1r, send_edges, lambda *rest: None)

    def pass_copy(d, w, slot):
        return pltpu.make_async_remote_copy(
            tedge.at[w, slot], tedge.at[w, slot], tf.at[d, slot], tr.at[w, slot],
            device_id=(sibling, b), device_id_type=MESH,
        )

    flat = gathered.reshape(16 * 256, 128)

    def put(plane, half, c, value):
        rows = pl.ds(pl.multiple_of(plane * 32 + 16 * half, 16), 16)
        high, low = split(value)
        fh[rows, 128 * c : 128 * c + 128] = high
        fl[rows, 128 * c : 128 * c + 128] = low

    @pl.loop(0, 32)
    def _(x):
        for half in range(2):
            for c in range(4):
                swapped = jnp.concatenate(
                    [flat[pl.ds(t * 2048 + x * 8 + half * 4 + c, 8, stride=256), :] for t in range(2)], axis=0
                )
                put(x + 8, half, c, jnp.where(turned, swapped, ec[c, x, 16 * half : 16 * half + 16, :]))

    image_load.wait()
    low_halo = pltpu.make_async_remote_copy(
        redge.at[pl.ds(0, 7)], rhalo.at[1], hs.at[0], hr.at[0],
        device_id=(v, (b + 15) % 16), device_id_type=MESH,
    )
    high_halo = pltpu.make_async_remote_copy(
        redge.at[pl.ds(9, 7)], rhalo.at[0], hs.at[1], hr.at[1],
        device_id=(v, (b + 1) % 16), device_id_type=MESH,
    )

    def ahead(g):
        rows = pl.ds(pl.multiple_of(g * 256, 256), 768)
        high, low = split(dot3(mfh[...], mfl[...], fh[rows, :], fl[rows, :]))
        blurred = dot3(high, low, tfh[...], tfl[...])
        ratio = image[pl.ds(8 * g, 8)].reshape(256, 512) / blurred
        high, low = split(ratio)
        inner = pl.ds(pl.multiple_of(g * 256 + 256, 256), 256)
        rh[inner, :] = high
        rl[inner, :] = low
        return ratio

    ahead(1)

    for slot in range(2):
        here = b > 0 if slot == 0 else b < 15
        there = b < 15 if slot == 0 else b > 0

        @pl.when(here)
        def _():
            for d in (0, 4, 3, 1, 2, 7, 5, 6):
                w = view_at(d % 4, d // 4)
                edge_copy(d, piece, w, slot).wait_recv()
                pass_copy(d, w, slot).start()

        @pl.when(there)
        def _():
            for d in range(8):
                edge_copy(d, piece, v, slot).wait_send()

    ahead(2)

    edge_flat = tedge.reshape(16 * 112, 128)

    @pl.when(has_before)
    def _():
        edge_pass.wait_send()

    @pl.when(has_after)
    def _():
        edge.wait_send()

    @pl.when(has_after)
    def _():
        pltpu.make_async_remote_copy(
            eh.at[1 - core], eh.at[1 - core], ef, er.at[1], device_id=(sibling, b), device_id_type=MESH
        ).wait_recv()

    for slot in range(2):
        here = b > 0 if slot == 0 else b < 15

        @pl.when(here)
        def _():
            for d in range(8):
                pass_copy(d, view_at(d % 4, d // 4), slot).wait_send()
                pass_copy(d, view_at(d % 4, d // 4, 1), slot).wait_recv()

            @pl.loop(0, 7)
            def _(x):
                for half in range(2):
                    for c in range(4):
                        start = slot * 56 + x * 8 + half * 4 + c
                        swapped = jnp.concatenate(
                            [edge_flat[pl.ds(t * 896 + start, 8, stride=112), :] for t in range(2)], axis=0
                        )
                        own = eh[slot, x, 16 * half : 16 * half + 16, 128 * c : 128 * c + 128]
                        put(x + 1 + 39 * slot, half, c, jnp.where(turned, swapped, own))

    @pl.loop(0, 2)
    def _(i):
        redge[pl.ds(8 * i, 8)] = ahead(3 * i).reshape(8, 32, 512)

        @pl.when((i == 0) & (b > 0))
        def _():
            low_halo.start()

        @pl.when((i == 1) & (b < 15))
        def _():
            high_halo.start()

    lflat = lp.reshape(16 * PIECE, 128)
    flag = jnp.full((8, 128), jnp.where(turned, 1.0, 0.0), F32)
    for w in range(16):
        lp[w, 0:8, :] = flag

    def back(g, place):
        rows = pl.ds(pl.multiple_of(g * 256, 256), 768)
        high, low = split(dot3(mah[...], mal[...], rh[rows, :], rl[rows, :]))
        correction[...] = dot3(high, low, tah[...], tal[...]).reshape(8, 32, 512)

        @pl.loop(0, 8)
        def _(k):
            seen = jnp.where(visible[0, g * 8 + k] == 1, 1.0, 0.0)
            for c in range(4):
                weight = jnp.where(turned, visrow[:, 128 * c : 128 * c + 128], jnp.full((8, 128), seen, F32))
                for t in range(4):
                    term = weight * jnp.log(correction[k, 8 * t : 8 * t + 8, 128 * c : 128 * c + 128])
                    start = (8 * (t % 2)) * PIECE + (place + k) * 8 + 8 + (t // 2) * 4 + c
                    lflat[pl.ds(start, 8, stride=PIECE), :] = term

    def direct(part, other, origin):
        rows = pl.ds(0, 136) if part == 0 else pl.ds(136, 128)
        return pltpu.make_async_remote_copy(
            lp.at[other, rows], rb.at[origin, rows], rs.at[part, other], rr.at[part, origin],
            device_id=(other, b), device_id_type=MESH,
        )

    def send_part(part):
        for which, order in ((0, [(1, 0, 0), (3, 0, 0), (0, 1, 0), (1, 0, 1), (3, 0, 1), (0, 1, 1), (2, 0, 0), (1, 1, 0), (3, 1, 0), (2, 0, 1), (1, 1, 1), (3, 1, 1), (2, 1, 0), (2, 1, 1), (0, 0, 1)]), (1, [(1, 1, 0), (3, 1, 0), (0, 1, 0), (2, 1, 0), (1, 1, 1), (3, 1, 1), (0, 1, 1), (2, 1, 1), (1, 0, 0), (3, 0, 0), (2, 0, 0), (1, 0, 1), (3, 0, 1), (2, 0, 1), (0, 0, 1)])):
            @pl.when(core == which)
            def _():
                for dx, dy, dc in order:
                    direct_to = view_at(dx, dy, dc)
                    direct(part, direct_to, v).start()

    @pl.loop(0, 2)
    def _(i):
        back(i + 1, 8 * i)

    send_part(0)

    def take_halo(slot):
        @pl.loop(0, 7)
        def _(t):
            high, low = split(rhalo[slot, t])
            rows = pl.ds(pl.multiple_of((t + 1 + 39 * slot) * 32, 32), 32)
            rh[rows, :] = high
            rl[rows, :] = low

    @pl.when(b > 0)
    def _():
        low_halo.wait_send()
        high_halo.wait_recv()
        take_halo(0)

    @pl.when(b < 15)
    def _():
        high_halo.wait_send()
        low_halo.wait_recv()
        take_halo(1)

    @pl.loop(0, 2)
    def _(i):
        back(3 * i, 16 + 8 * i)

    send_part(1)

    def sums(z, place):
        rows = pl.ds(pl.multiple_of(place * 8 + 8, 8), 8)
        up = jnp.zeros((8, 128), F32)
        tp = jnp.zeros((8, 128), F32)
        for w in range(16):
            term = rb[w, rows, :]
            share = term * rb[w, 0:8, :]
            tp = tp + share
            up = up + (term - share)
        rows = pl.ds(pl.multiple_of(z * 8, 8), 8)
        upiece[rows, :] = up
        tpiece[rows, :] = tp

    def take_part(part):
        @pl.loop(0, 17 - part)
        def _(t):
            rows = pl.ds(pl.multiple_of(t * 8 + 136 * part, 8), 8)
            rb.at[v][rows, :] = lp.at[v][rows, :]

        @pl.loop(1, 16)
        def _(d):
            other = (v + d) % 16
            direct(part, other, other).wait_recv()

    take_part(0)

    @pl.loop(0, 16)
    def _(t):
        sums(t + 8, t)

    take_part(1)

    @pl.loop(0, 16)
    def _(t):
        sums(t + 16 * (t // 8), t + 16)

    for part in range(2):
        @pl.loop(1, 16)
        def _(d):
            other = (v + d) % 16
            direct(part, other, other).wait_send()

    make_messages(lambda half, c: tpiece[pl.ds(half * 4 + c, 32, stride=8), :], sbox2)
    exchange(sbox2, rbox2, a2s, a2r)
    take_messages(rbox2, ttpiece)
    upiece[...] = epiece[...] * jnp.exp((upiece[...] + ttpiece[...]) * (1.0 / 16.0))

    def out_copy(ref, w, rows, half):
        return pltpu.make_async_copy(ref.at[rows], o_hbm.at[w, rows], os.at[w, half])

    gather(
        upiece, gathered2, g2s, g2r,
        lambda d, ref, w, rows, half: out_copy(ref, w, rows, half).start(),
        lambda ref, w, rows, half: out_copy(ref, w, rows, half).start(),
    )

    @pl.loop(0, 16)
    def _(w):
        for half in range(2):
            out_copy(upiece, w, pl.ds(128 * half, 128), half).wait()


def reorder(pieces, out):
    flat = pieces.reshape(16 * 128, 128)

    @pl.loop(0, 16)
    def _(x):
        for t in range(4):
            for c in range(4):
                start = (8 * (t % 2)) * 128 + x * 8 + (t // 2) * 4 + c
                out[x, 8 * t : 8 * t + 8, 128 * c : 128 * c + 128] = flat[pl.ds(start, 8, stride=128), :]


def shards(estimate, image, psf, perm, shift, visible):
    smem = pl.BlockSpec(memory_space=pltpu.SMEM)
    hbm = pl.BlockSpec(memory_space=pl.ANY)
    vmem = pltpu.VMEM
    dma = pltpu.SemaphoreType.DMA
    pieces = pl.pallas_call(
        kernel,
        out_shape=jax.ShapeDtypeStruct((16, 256, 128), F32),
        in_specs=[hbm] + [smem] * 3 + [hbm] * 2,
        out_specs=hbm,
        scratch_shapes=[
            pltpu.SMEM((3, 1, 15), F32),
            vmem((4, 32, 32, 128), F32),
            vmem((32, 32, 512), F32),
            vmem((2, 7, 32, 512), F32),
            vmem((16, 2, 56, 128), F32),
        ]
        + [vmem((1536, 512), BF16)] * 4
        + [vmem((16, 32, 512), F32), vmem((2, 7, 32, 512), F32)]
        + [vmem((256, 768), BF16)] * 4
        + [vmem((512, 512), BF16)] * 4
        + [
            vmem((16, 3, 8, 128), F32),
            vmem((16, 3, 8, 128), F32),
            vmem((16, 2, 8, 128), F32),
            vmem((16, 2, 8, 128), F32),
            vmem((8, 512), F32),
            vmem((256, 128), F32),
            vmem((256, 128), F32),
            vmem((16, 256, 128), F32),
            vmem((8, 32, 512), F32),
            vmem((16, PIECE, 128), F32),
            vmem((16, PIECE, 128), F32),
            vmem((256, 128), F32),
            vmem((256, 128), F32),
            vmem((256, 128), F32),
            vmem((16, 256, 128), F32),
            dma((6,)),
            dma((16, 2)),
        ]
        + [dma((16,))] * 4
        + [dma((30,)), dma((16, 2))] * 2
        + [dma, dma((2,)), dma]
        + [dma((8, 2)), dma((16, 2)), dma((8, 2))]
        + [dma((2,)), dma((2,)), dma((2, 16)), dma((2, 16))],
        compiler_params=pltpu.CompilerParams(
            collective_id=0, has_side_effects=True, vmem_limit_bytes=60 * 1024 * 1024
        ),
    )(jnp.transpose(psf, (1, 0, 2)), perm, shift, visible, estimate, image)
    return pl.pallas_call(
        reorder,
        out_shape=jax.ShapeDtypeStruct(estimate.shape, F32),
        grid=(2,),
        in_specs=[pl.BlockSpec((16, 128, 128), lambda i: (0, i, 0))],
        out_specs=pl.BlockSpec((16, 32, 512), lambda i: (i, 0, 0)),
    )(pieces)


def solution(mesh):
    placed = (
        P("bulk", None, None),
        P("view", "bulk", None, None),
        P("view", None, None),
        P("view"),
        P("view"),
        P("view", "bulk"),
    )
    return jax.shard_map(
        shards, mesh=mesh, in_specs=placed, out_specs=P("bulk", None, None), check_vma=False
    )
```

```python
import jax
import jax.numpy as jnp
from jax import lax
from jax.experimental import pallas as pl
from jax.experimental.pallas import tpu as pltpu
from jax.sharding import PartitionSpec as P

MESH = pl.DeviceIdType.MESH
F32 = jnp.float32
BF16 = jnp.bfloat16
PIECE = 33 * 8


def split(x):
    high = x.astype(BF16)
    return high, (x - high.astype(F32)).astype(BF16)


def dot3(ah, al, bh, bl):
    def dot(a, b):
        return lax.dot_general(a, b, (((1,), (0,)), ((), ())), preferred_element_type=F32)

    return dot(ah, bh) + dot(ah, bl) + dot(al, bh)


def lane_groups(ins):
    group = lax.broadcasted_iota(jnp.int32, (8, 128), 1) >> 5
    outs = []
    for i in range(4):
        out = ins[i]
        for j in range(4):
            if j != i:
                out = jnp.where(group == j, pltpu.roll(ins[j], (32 * (j - i)) % 128, 1), out)
        outs.append(out)
    return outs


def make_messages(load, box):
    for half in range(2):
        stacked = jnp.concatenate([load(half, c) for c in range(4)], axis=0)
        turned = stacked.T
        for r in range(4):
            outs = lane_groups([turned[r * 32 + q * 8 : r * 32 + q * 8 + 8] for q in range(4)])
            for c in range(4):
                box[4 * c + r, half] = outs[c]


def take_messages(box, piece):
    for half in range(2):
        for c in range(4):
            outs = lane_groups([box[4 * c + r, half] for r in range(4)])
            for q in range(4):
                piece[pl.ds(q * 64 + half * 4 + c, 8, stride=8), :] = outs[q]


ORDER = (
    (1, 0, 0), (3, 0, 0), (0, 1, 0), (1, 0, 1), (3, 0, 1), (0, 1, 1), (2, 0, 0), (1, 1, 0),
    (3, 1, 0), (2, 0, 1), (1, 1, 1), (3, 1, 1), (2, 1, 0), (2, 1, 1), (0, 0, 1),
)


def kernel(
    psf_hbm, perm, shift, visible, e_hbm, i_hbm, o_hbm,
    psf, ec, image, eh, tedge, fh, fl, rh, rl, redge, rhalo, mfh, mfl, mah, mal, tfh, tfl, tah, tal,
    sbox, rbox, sbox2, rbox2, visrow, epiece, piece, gathered, correction, lp, rb,
    upiece, tpiece, ttpiece, gathered2,
    local_sem, os, a1s, a1r, a2s, a2r, g1s, g1r, g2s, g2r, es, er, ef, ts, tr, tf, hs, hr, rs, rr,
):
    v = lax.axis_index("view")
    b = lax.axis_index("bulk")
    core = v % 2
    chip = v // 2
    sibling = v + 1 - 2 * core
    column = chip % 4
    side = chip // 4

    def view_at(dx, dy, dc=0):
        return (side + dy - 2 * dy * side) * 8 + ((column + dx) % 4) * 2 + core + dc - 2 * dc * core


    psf_load = pltpu.make_async_copy(psf_hbm, psf, local_sem.at[5])
    psf_load.start()
    loads = [
        pltpu.make_async_copy(e_hbm.at[:, :, pl.ds(128 * c, 128)], ec.at[c], local_sem.at[c])
        for c in range(4)
    ]
    image_load = pltpu.make_async_copy(i_hbm.at[0], image, local_sem.at[4])
    for load in loads:
        load.start()
    image_load.start()

    barrier = pltpu.get_barrier_semaphore()

    @pl.loop(1, 16)
    def _(d):
        pl.semaphore_signal(barrier, inc=1, device_id=((v + d) % 16, b), device_id_type=MESH)
        pl.semaphore_signal(barrier, inc=1, device_id=(v, (b + d) % 16), device_id_type=MESH)

    turned = perm[0] == 1
    moved = shift[0]

    vlane = lax.broadcasted_iota(jnp.int32, (8, 128), 1) & 31
    vtile = jnp.zeros((8, 128), F32)
    for t in range(32):
        vtile = jnp.where(vlane == t, jnp.where(visible[0, t] == 1, 1.0, 0.0), vtile)

    for load in loads:
        load.wait()

    erows_flat = ec.reshape(4 * 1024, 128)

    def erows(half, c):
        return erows_flat[pl.ds(1024 * c + v + 16 * half, 32, stride=32), :]

    for half in range(2):
        for c in range(4):
            epiece[pl.ds(half * 4 + c, 32, stride=8), :] = erows(half, c)
    make_messages(erows, sbox)
    for t in range(16):
        sbox[t, 2] = vtile

    pl.semaphore_wait(barrier, 30)

    after = b + 1 - 2 * core
    before = b - 1 + 2 * core
    has_after = (after >= 0) & (after < 16)
    has_before = (before >= 0) & (before < 16)
    edge = pltpu.make_async_remote_copy(
        e_hbm.at[pl.ds(25 * (1 - core), 7)], eh.at[core], es, er.at[0], device_id=(v, (after + 16) % 16), device_id_type=MESH
    )

    def exchange(source, target, send, recv, between=None):
        @pl.loop(1, 16)
        def _(d):
            other = (b + 16 + d * (1 - 2 * core)) % 16
            pltpu.make_async_remote_copy(
                source.at[other], target.at[b], send.at[other], recv.at[b],
                device_id=(v, other), device_id_type=MESH,
            ).start()

        if between is not None:
            between()
        target[b] = source[b]

        @pl.loop(1, 16)
        def _(d):
            other = (b + d) % 16
            copy = pltpu.make_async_remote_copy(
                source.at[other], target.at[other], send.at[other], recv.at[other],
                device_id=(v, other), device_id_type=MESH,
            )
            copy.wait_send()
            copy.wait_recv()

    def start_edge():
        @pl.when(has_after)
        def _():
            edge.start()

        psf_load.wait()

        row = lax.broadcasted_iota(jnp.int32, (32, 128), 0)
        lane = lax.broadcasted_iota(jnp.int32, (32, 128), 1)

        def pick(index, axis, reverse, shape):
            total = psf[axis, 0, 0]
            for t in range(1, 15):
                total = total + psf[axis, 0, t]
            out = jnp.zeros(shape, F32)
            for t in range(15):
                out = jnp.where(index == t, psf[axis, 0, 14 - t if reverse else t], out)
            return out / jnp.full(shape, total, F32)

        zlane = lax.broadcasted_iota(jnp.int32, (8, 768), 1) >> 5
        brow = lax.broadcasted_iota(jnp.int32, (128, 128), 0)
        blane = lax.broadcasted_iota(jnp.int32, (128, 128), 1)
        for reverse, mh, ml, th, tl in ((False, mfh, mfl, tfh, tfl), (True, mah, mal, tah, tal)):
            offset = -moved if reverse else moved
            circ = pick(((lane & 31) - row + 7 + offset) & 31, 1, reverse, (32, 128))
            wide = jnp.concatenate([circ] * 6, axis=1)
            for zo in range(8):
                zrow = pick(zlane - zo - 1, 0, reverse, (8, 768))
                high, low = split(wide * zrow[0:1])
                mh[zo * 32 : zo * 32 + 32, :] = high
                ml[zo * 32 : zo * 32 + 32, :] = low
            th[...] = jnp.zeros((512, 512), BF16)
            tl[...] = jnp.zeros((512, 512), BF16)
            for delta in (-1, 0, 1):
                high, low = split(pick(brow - blane - 128 * delta + 7, 2, reverse, (128, 128)))
                for i in range(4):
                    j = i + delta
                    if 0 <= j < 4:
                        th[i * 128 : i * 128 + 128, j * 128 : j * 128 + 128] = high
                        tl[i * 128 : i * 128 + 128, j * 128 : j * 128 + 128] = low

        zero = jnp.zeros((32, 512), BF16)
        for ref in (fh, fl, rh, rl):
            ref[0:32, :] = zero
            ref[1504:1536, :] = zero

            @pl.when(b == 0)
            def _():
                for t in range(1, 8):
                    ref[t * 32 : t * 32 + 32, :] = zero

            @pl.when(b == 15)
            def _():
                for t in range(40, 47):
                    ref[t * 32 : t * 32 + 32, :] = zero

    exchange(sbox, rbox, a1s, a1r, start_edge)

    take_messages(rbox, piece)
    group = lax.broadcasted_iota(jnp.int32, (8, 128), 1) >> 5
    for c in range(4):
        seen = rbox[4 * c, 2]
        for q in range(1, 4):
            seen = jnp.where(group == q, rbox[4 * c + q, 2], seen)
        visrow[:, 128 * c : 128 * c + 128] = seen

    def gather(own, everything, send, recv, on_half, on_passed):
        used = []

        def place(h):
            return (h + core) % 2

        def rows(h):
            return pl.ds(pl.multiple_of(128 * place(h), 128), 128)

        def push(w, h, target, source=None):
            copy = pltpu.make_async_remote_copy(
                (everything.at[w] if source is None else source).at[rows(h)], everything.at[w, rows(h)],
                send.at[len(used)], recv.at[w, place(h)], device_id=(target, b), device_id_type=MESH,
            )
            copy.start()
            used.append(copy)

        def landed(w, h):
            pltpu.make_async_remote_copy(
                own.at[rows(h)], everything.at[w, rows(h)], send.at[0], recv.at[w, place(h)],
                device_id=(sibling, b), device_id_type=MESH,
            ).wait_recv()

        right, left, across, far = view_at(1, 0), view_at(3, 0), view_at(0, 1), view_at(2, 0)
        for first, second in ((across, right), (right, left), (left, far), (far, across)):
            push(v, 0, first, own)
            push(v, 1, second, own)
        for h in range(2):
            push(v, h, sibling, own)
            on_half(0, own, v, rows(h), place(h))

        @pl.loop(0, 32)
        def _(t):
            tile = pl.ds(pl.multiple_of(t * 8, 8), 8)
            everything.at[v][tile, :] = own[tile, :]

        def relay(dx, dy, h, targets):
            w = view_at(dx, dy)
            landed(w, h)
            for target in targets:
                push(w, h, target)
            push(w, h, sibling)
            on_half(dx + 4 * dy, everything.at[w], w, rows(h), place(h))

        relay(0, 1, 0, (right, left, far))
        relay(3, 0, 1, (across,))
        relay(1, 0, 1, (across,))
        relay(3, 0, 0, ())
        relay(1, 0, 0, ())
        relay(2, 0, 1, (across,))
        relay(2, 0, 0, ())
        relay(0, 1, 1, ())
        for dx in (3, 1, 2):
            for h in range(2):
                relay(dx, 1, h, ())

        for dy in range(2):
            for dx in range(4):
                w = view_at(dx, dy, 1)
                for h in range(2):
                    landed(w, h)
                    on_passed(everything.at[w], w, rows(h), place(h))

        for copy in used:
            copy.wait_send()

    def edge_copy(d, ref, w, slot):
        return pltpu.make_async_remote_copy(
            ref.at[pl.ds(200 * (1 - slot), 56)], tedge.at[w, slot], ts.at[d, slot], tr.at[w, slot],
            device_id=(v, (b + 17 - 2 * slot) % 16), device_id_type=MESH,
        )

    edge_pass = pltpu.make_async_remote_copy(
        eh.at[core], eh.at[core], ef, er.at[1], device_id=(sibling, b), device_id_type=MESH
    )

    halves = []

    def send_edges(d, ref, w, rows, half):
        target = b - 1 + 2 * half

        @pl.when((target >= 0) & (target < 16))
        def _():
            edge_copy(d, ref, w, 1 - half).start()

        halves.append(d)
        if len(halves) == 8:

            @pl.when(has_before)
            def _():
                edge.wait_recv()
                edge_pass.start()

    gather(piece, gathered, g1s, g1r, send_edges, lambda *rest: None)

    def pass_copy(d, w, slot):
        return pltpu.make_async_remote_copy(
            tedge.at[w, slot], tedge.at[w, slot], tf.at[d, slot], tr.at[w, slot],
            device_id=(sibling, b), device_id_type=MESH,
        )

    flat = gathered.reshape(16 * PIECE, 128)

    def put(plane, half, c, value):
        rows = pl.ds(pl.multiple_of(plane * 32 + 16 * half, 16), 16)
        high, low = split(value)
        fh[rows, 128 * c : 128 * c + 128] = high
        fl[rows, 128 * c : 128 * c + 128] = low

    @pl.loop(0, 32)
    def _(x):
        for half in range(2):
            for c in range(4):
                swapped = jnp.concatenate(
                    [flat[pl.ds(t * 8 * PIECE + x * 8 + half * 4 + c, 8, stride=PIECE), :] for t in range(2)], axis=0
                )
                put(x + 8, half, c, jnp.where(turned, swapped, ec[c, x, 16 * half : 16 * half + 16, :]))

    image_load.wait()
    low_halo = pltpu.make_async_remote_copy(
        redge.at[pl.ds(0, 7)], rhalo.at[1], hs.at[0], hr.at[0],
        device_id=(v, (b + 15) % 16), device_id_type=MESH,
    )
    high_halo = pltpu.make_async_remote_copy(
        redge.at[pl.ds(9, 7)], rhalo.at[0], hs.at[1], hr.at[1],
        device_id=(v, (b + 1) % 16), device_id_type=MESH,
    )

    def ahead(g):
        rows = pl.ds(pl.multiple_of(g * 256, 256), 768)
        high, low = split(dot3(mfh[...], mfl[...], fh[rows, :], fl[rows, :]))
        blurred = dot3(high, low, tfh[...], tfl[...])
        ratio = image[pl.ds(8 * g, 8)].reshape(256, 512) / blurred
        high, low = split(ratio)
        inner = pl.ds(pl.multiple_of(g * 256 + 256, 256), 256)
        rh[inner, :] = high
        rl[inner, :] = low
        return ratio

    ahead(1)

    for slot in range(2):
        here = b > 0 if slot == 0 else b < 15
        there = b < 15 if slot == 0 else b > 0

        @pl.when(here)
        def _():
            for d in (0, 4, 3, 1, 2, 7, 5, 6):
                w = view_at(d % 4, d // 4)
                edge_copy(d, piece, w, slot).wait_recv()
                pass_copy(d, w, slot).start()

        @pl.when(there)
        def _():
            for d in range(8):
                edge_copy(d, piece, v, slot).wait_send()

    ahead(2)

    edge_flat = tedge.reshape(16 * 112, 128)

    @pl.when(has_before)
    def _():
        edge_pass.wait_send()

    @pl.when(has_after)
    def _():
        edge.wait_send()

    @pl.when(has_after)
    def _():
        pltpu.make_async_remote_copy(
            eh.at[1 - core], eh.at[1 - core], ef, er.at[1], device_id=(sibling, b), device_id_type=MESH
        ).wait_recv()

    for slot in range(2):
        here = b > 0 if slot == 0 else b < 15

        @pl.when(here)
        def _():
            for d in range(8):
                pass_copy(d, view_at(d % 4, d // 4), slot).wait_send()
                pass_copy(d, view_at(d % 4, d // 4, 1), slot).wait_recv()

            @pl.loop(0, 7)
            def _(x):
                for half in range(2):
                    for c in range(4):
                        start = slot * 56 + x * 8 + half * 4 + c
                        swapped = jnp.concatenate(
                            [edge_flat[pl.ds(t * 896 + start, 8, stride=112), :] for t in range(2)], axis=0
                        )
                        own = eh[slot, x, 16 * half : 16 * half + 16, 128 * c : 128 * c + 128]
                        put(x + 1 + 39 * slot, half, c, jnp.where(turned, swapped, own))

    @pl.loop(0, 2)
    def _(i):
        redge[pl.ds(8 * i, 8)] = ahead(3 * i).reshape(8, 32, 512)

        @pl.when((i == 0) & (b > 0))
        def _():
            low_halo.start()

        @pl.when((i == 1) & (b < 15))
        def _():
            high_halo.start()

    lflat = lp.reshape(16 * PIECE, 128)
    flag = jnp.full((8, 128), jnp.where(turned, 1.0, 0.0), F32)
    for w in range(16):
        lp[w, 0:8, :] = flag

    def back(g, place):
        rows = pl.ds(pl.multiple_of(g * 256, 256), 768)
        high, low = split(dot3(mah[...], mal[...], rh[rows, :], rl[rows, :]))
        correction[...] = dot3(high, low, tah[...], tal[...]).reshape(8, 32, 512)

        @pl.loop(0, 8)
        def _(k):
            seen = jnp.where(visible[0, g * 8 + k] == 1, 1.0, 0.0)
            for c in range(4):
                weight = jnp.where(turned, visrow[:, 128 * c : 128 * c + 128], jnp.full((8, 128), seen, F32))
                for t in range(4):
                    term = weight * jnp.log(correction[k, 8 * t : 8 * t + 8, 128 * c : 128 * c + 128])
                    start = (8 * (t % 2)) * PIECE + (place + k) * 8 + 8 + (t // 2) * 4 + c
                    lflat[pl.ds(start, 8, stride=PIECE), :] = term

    def direct(part, other, origin):
        rows = pl.ds(0, 136) if part == 0 else pl.ds(136, 128)
        return pltpu.make_async_remote_copy(
            lp.at[other, rows], rb.at[origin, rows], rs.at[part, other], rr.at[part, origin],
            device_id=(other, b), device_id_type=MESH,
        )

    def send_part(part):
        for which, order in ((0, [(1, 0, 0), (3, 0, 0), (0, 1, 0), (1, 0, 1), (3, 0, 1), (0, 1, 1), (2, 0, 0), (1, 1, 0), (3, 1, 0), (2, 0, 1), (1, 1, 1), (3, 1, 1), (2, 1, 0), (2, 1, 1), (0, 0, 1)]), (1, [(1, 1, 0), (3, 1, 0), (0, 1, 0), (2, 1, 0), (1, 1, 1), (3, 1, 1), (0, 1, 1), (2, 1, 1), (1, 0, 0), (3, 0, 0), (2, 0, 0), (1, 0, 1), (3, 0, 1), (2, 0, 1), (0, 0, 1)])):
            @pl.when(core == which)
            def _():
                for dx, dy, dc in order:
                    direct_to = view_at(dx, dy, dc)
                    direct(part, direct_to, v).start()

    @pl.loop(0, 2)
    def _(i):
        back(i + 1, 8 * i)

    send_part(0)

    def take_halo(slot):
        @pl.loop(0, 7)
        def _(t):
            high, low = split(rhalo[slot, t])
            rows = pl.ds(pl.multiple_of((t + 1 + 39 * slot) * 32, 32), 32)
            rh[rows, :] = high
            rl[rows, :] = low

    @pl.when(b > 0)
    def _():
        low_halo.wait_send()
        high_halo.wait_recv()
        take_halo(0)

    @pl.when(b < 15)
    def _():
        high_halo.wait_send()
        low_halo.wait_recv()
        take_halo(1)

    @pl.loop(0, 2)
    def _(i):
        back(3 * i, 16 + 8 * i)

    send_part(1)

    def sums(z, place):
        rows = pl.ds(pl.multiple_of(place * 8 + 8, 8), 8)
        up = jnp.zeros((8, 128), F32)
        tp = jnp.zeros((8, 128), F32)
        for w in range(16):
            term = rb[w, rows, :]
            share = term * rb[w, 0:8, :]
            tp = tp + share
            up = up + (term - share)
        rows = pl.ds(pl.multiple_of(z * 8, 8), 8)
        upiece[rows, :] = up
        tpiece[rows, :] = tp

    def take_part(part):
        @pl.loop(0, 17 - part)
        def _(t):
            rows = pl.ds(pl.multiple_of(t * 8 + 136 * part, 8), 8)
            rb.at[v][rows, :] = lp.at[v][rows, :]

        @pl.loop(1, 16)
        def _(d):
            other = (v + d) % 16
            direct(part, other, other).wait_recv()

    take_part(0)

    @pl.loop(0, 16)
    def _(t):
        sums(t + 8, t)

    take_part(1)

    @pl.loop(0, 16)
    def _(t):
        sums(t + 16 * (t // 8), t + 16)

    for part in range(2):
        @pl.loop(1, 16)
        def _(d):
            other = (v + d) % 16
            direct(part, other, other).wait_send()

    make_messages(lambda half, c: tpiece[pl.ds(half * 4 + c, 32, stride=8), :], sbox2)
    exchange(sbox2, rbox2, a2s, a2r)
    take_messages(rbox2, ttpiece)
    upiece[...] = epiece[...] * jnp.exp((upiece[...] + ttpiece[...]) * (1.0 / 16.0))

    def out_copy(ref, w, rows, half):
        return pltpu.make_async_copy(ref.at[rows], o_hbm.at[w, rows], os.at[w, half])

    gather(
        upiece, gathered2, g2s, g2r,
        lambda d, ref, w, rows, half: out_copy(ref, w, rows, half).start(),
        lambda ref, w, rows, half: out_copy(ref, w, rows, half).start(),
    )

    @pl.loop(0, 16)
    def _(w):
        for half in range(2):
            out_copy(upiece, w, pl.ds(128 * half, 128), half).wait()


def reorder(p_hbm, o_hbm, pieces, out, sem_in, sem_out):
    loads, stores = [], []
    for i in range(4):
        part = pl.ds(64 * i, 64)
        loads.append(pltpu.make_async_copy(p_hbm.at[:, part], pieces.at[:, part, :], sem_in.at[i]))
        stores.append(pltpu.make_async_copy(out.at[pl.ds(8 * i, 8)], o_hbm.at[pl.ds(8 * i, 8)], sem_out.at[i]))
    for load in loads:
        load.start()
    flat = pieces.reshape(16 * PIECE, 128)
    for i in range(4):
        loads[i].wait()

        @pl.loop(8 * i, 8 * i + 8)
        def _(z):
            for t in range(4):
                for c in range(4):
                    start = (8 * (t % 2)) * PIECE + z * 8 + (t // 2) * 4 + c
                    out[z, 8 * t : 8 * t + 8, 128 * c : 128 * c + 128] = flat[pl.ds(start, 8, stride=PIECE), :]

        stores[i].start()
    for store in stores:
        store.wait()


def shards(estimate, image, psf, perm, shift, visible):
    smem = pl.BlockSpec(memory_space=pltpu.SMEM)
    hbm = pl.BlockSpec(memory_space=pl.ANY)
    vmem = pltpu.VMEM
    dma = pltpu.SemaphoreType.DMA
    pieces = pl.pallas_call(
        kernel,
        out_shape=jax.ShapeDtypeStruct((16, 256, 128), F32),
        in_specs=[hbm] + [smem] * 3 + [hbm] * 2,
        out_specs=hbm,
        scratch_shapes=[
            pltpu.SMEM((3, 1, 15), F32),
            vmem((4, 32, 32, 128), F32),
            vmem((32, 32, 512), F32),
            vmem((2, 7, 32, 512), F32),
            vmem((16, 2, 56, 128), F32),
        ]
        + [vmem((1536, 512), BF16)] * 4
        + [vmem((16, 32, 512), F32), vmem((2, 7, 32, 512), F32)]
        + [vmem((256, 768), BF16)] * 4
        + [vmem((512, 512), BF16)] * 4
        + [
            vmem((16, 3, 8, 128), F32),
            vmem((16, 3, 8, 128), F32),
            vmem((16, 2, 8, 128), F32),
            vmem((16, 2, 8, 128), F32),
            vmem((8, 512), F32),
            vmem((256, 128), F32),
            vmem((256, 128), F32),
            vmem((16, PIECE, 128), F32),
            vmem((8, 32, 512), F32),
            vmem((16, PIECE, 128), F32),
            vmem((16, PIECE, 128), F32),
            vmem((256, 128), F32),
            vmem((256, 128), F32),
            vmem((256, 128), F32),
            vmem((16, 256, 128), F32),
            dma((6,)),
            dma((16, 2)),
        ]
        + [dma((16,))] * 4
        + [dma((30,)), dma((16, 2))] * 2
        + [dma, dma((2,)), dma]
        + [dma((8, 2)), dma((16, 2)), dma((8, 2))]
        + [dma((2,)), dma((2,)), dma((2, 16)), dma((2, 16))],
        compiler_params=pltpu.CompilerParams(
            collective_id=0, has_side_effects=True, vmem_limit_bytes=60 * 1024 * 1024
        ),
    )(jnp.transpose(psf, (1, 0, 2)), perm, shift, visible, estimate, image)
    return pl.pallas_call(
        reorder,
        out_shape=jax.ShapeDtypeStruct(estimate.shape, F32),
        in_specs=[hbm],
        out_specs=hbm,
        scratch_shapes=[vmem((16, PIECE, 128), F32), vmem((32, 32, 512), F32), dma((4,)), dma((4,))],
    )(pieces)


def solution(mesh):
    placed = (
        P("bulk", None, None),
        P("view", "bulk", None, None),
        P("view", None, None),
        P("view"),
        P("view"),
        P("view", "bulk"),
    )
    return jax.shard_map(
        shards, mesh=mesh, in_specs=placed, out_specs=P("bulk", None, None), check_vma=False
    )
```

```python
import jax
import jax.numpy as jnp
from jax import lax
from jax.experimental import pallas as pl
from jax.experimental.pallas import tpu as pltpu
from jax.sharding import PartitionSpec as P

MESH = pl.DeviceIdType.MESH
F32 = jnp.float32
BF16 = jnp.bfloat16
PIECE = 33 * 8


def split(x):
    high = x.astype(BF16)
    return high, (x - high.astype(F32)).astype(BF16)


def dot3(ah, al, bh, bl):
    def dot(a, b):
        return lax.dot_general(a, b, (((1,), (0,)), ((), ())), preferred_element_type=F32)

    return dot(ah, bh) + dot(ah, bl) + dot(al, bh)


def lane_groups(ins):
    group = lax.broadcasted_iota(jnp.int32, (8, 128), 1) >> 5
    outs = []
    for i in range(4):
        out = ins[i]
        for j in range(4):
            if j != i:
                out = jnp.where(group == j, pltpu.roll(ins[j], (32 * (j - i)) % 128, 1), out)
        outs.append(out)
    return outs


def make_messages(load, box):
    for half in range(2):
        stacked = jnp.concatenate([load(half, c) for c in range(4)], axis=0)
        turned = stacked.T
        for r in range(4):
            outs = lane_groups([turned[r * 32 + q * 8 : r * 32 + q * 8 + 8] for q in range(4)])
            for c in range(4):
                box[4 * c + r, half] = outs[c]


def take_messages(box, piece):
    for half in range(2):
        for c in range(4):
            outs = lane_groups([box[4 * c + r, half] for r in range(4)])
            for q in range(4):
                piece[pl.ds(q * 64 + half * 4 + c, 8, stride=8), :] = outs[q]


ORDER = (
    (1, 0, 0), (3, 0, 0), (0, 1, 0), (1, 0, 1), (3, 0, 1), (0, 1, 1), (2, 0, 0), (1, 1, 0),
    (3, 1, 0), (2, 0, 1), (1, 1, 1), (3, 1, 1), (2, 1, 0), (2, 1, 1), (0, 0, 1),
)


def kernel(
    psf_hbm, perm, shift, visible, e_hbm, i_hbm, o_hbm,
    psf, ec, image, eh, tedge, fh, fl, rh, rl, redge, rhalo, mfh, mfl, mah, mal, tfh, tfl, tah, tal,
    sbox, rbox, sbox2, rbox2, visrow, epiece, piece, gathered, correction, lp, rb,
    upiece, tpiece, ttpiece, gathered2,
    local_sem, os, a1s, a1r, a2s, a2r, g1s, g1r, g2s, g2r, es, er, ef, ts, tr, tf, hs, hr, rs, rr,
):
    v = lax.axis_index("view")
    b = lax.axis_index("bulk")
    core = v % 2
    chip = v // 2
    sibling = v + 1 - 2 * core
    column = chip % 4
    side = chip // 4

    def view_at(dx, dy, dc=0):
        return (side + dy - 2 * dy * side) * 8 + ((column + dx) % 4) * 2 + core + dc - 2 * dc * core


    psf_load = pltpu.make_async_copy(psf_hbm, psf, local_sem.at[5])
    psf_load.start()
    loads = [
        pltpu.make_async_copy(e_hbm.at[:, :, pl.ds(128 * c, 128)], ec.at[c], local_sem.at[c])
        for c in range(4)
    ]
    image_load = pltpu.make_async_copy(i_hbm.at[0], image, local_sem.at[4])
    for load in loads:
        load.start()
    image_load.start()

    barrier = pltpu.get_barrier_semaphore()

    @pl.loop(1, 16)
    def _(d):
        pl.semaphore_signal(barrier, inc=1, device_id=((v + d) % 16, b), device_id_type=MESH)
        pl.semaphore_signal(barrier, inc=1, device_id=(v, (b + d) % 16), device_id_type=MESH)

    turned = perm[0] == 1
    moved = shift[0]

    vlane = lax.broadcasted_iota(jnp.int32, (8, 128), 1) & 31
    vtile = jnp.zeros((8, 128), F32)
    for t in range(32):
        vtile = jnp.where(vlane == t, jnp.where(visible[0, t] == 1, 1.0, 0.0), vtile)

    for load in loads:
        load.wait()

    erows_flat = ec.reshape(4 * 1024, 128)

    def erows(half, c):
        return erows_flat[pl.ds(1024 * c + v + 16 * half, 32, stride=32), :]

    for half in range(2):
        for c in range(4):
            epiece[pl.ds(half * 4 + c, 32, stride=8), :] = erows(half, c)
    make_messages(erows, sbox)
    for t in range(16):
        sbox[t, 2] = vtile

    pl.semaphore_wait(barrier, 30)

    after = b + 1 - 2 * core
    before = b - 1 + 2 * core
    has_after = (after >= 0) & (after < 16)
    has_before = (before >= 0) & (before < 16)
    edge = pltpu.make_async_remote_copy(
        e_hbm.at[pl.ds(25 * (1 - core), 7)], eh.at[core], es, er.at[0], device_id=(v, (after + 16) % 16), device_id_type=MESH
    )

    def exchange(source, target, send, recv, between=None):
        @pl.loop(1, 16)
        def _(d):
            other = (b + 16 + d * (1 - 2 * core)) % 16
            pltpu.make_async_remote_copy(
                source.at[other], target.at[b], send.at[other], recv.at[b],
                device_id=(v, other), device_id_type=MESH,
            ).start()

        if between is not None:
            between()
        target[b] = source[b]

        @pl.loop(1, 16)
        def _(d):
            other = (b + d) % 16
            copy = pltpu.make_async_remote_copy(
                source.at[other], target.at[other], send.at[other], recv.at[other],
                device_id=(v, other), device_id_type=MESH,
            )
            copy.wait_recv()

        @pl.loop(1, 16)
        def _(d):
            other = (b + d) % 16
            pltpu.make_async_remote_copy(
                source.at[other], target.at[other], send.at[other], recv.at[other],
                device_id=(v, other), device_id_type=MESH,
            ).wait_send()

    def build(group):
        row = lax.broadcasted_iota(jnp.int32, (32, 128), 0)
        lane = lax.broadcasted_iota(jnp.int32, (32, 128), 1)

        def pick(index, axis, reverse, shape):
            total = psf[axis, 0, 0]
            for t in range(1, 15):
                total = total + psf[axis, 0, t]
            out = jnp.zeros(shape, F32)
            for t in range(15):
                out = jnp.where(index == t, psf[axis, 0, 14 - t if reverse else t], out)
            return out / jnp.full(shape, total, F32)

        zlane = lax.broadcasted_iota(jnp.int32, (8, 768), 1) >> 5
        brow = lax.broadcasted_iota(jnp.int32, (128, 128), 0)
        blane = lax.broadcasted_iota(jnp.int32, (128, 128), 1)
        for reverse, mh, ml, th, tl in (group,):
            offset = -moved if reverse else moved
            circ = pick(((lane & 31) - row + 7 + offset) & 31, 1, reverse, (32, 128))
            wide = jnp.concatenate([circ] * 6, axis=1)
            for zo in range(8):
                zrow = pick(zlane - zo - 1, 0, reverse, (8, 768))
                high, low = split(wide * zrow[0:1])
                mh[zo * 32 : zo * 32 + 32, :] = high
                ml[zo * 32 : zo * 32 + 32, :] = low
            th[...] = jnp.zeros((512, 512), BF16)
            tl[...] = jnp.zeros((512, 512), BF16)
            for delta in (-1, 0, 1):
                high, low = split(pick(brow - blane - 128 * delta + 7, 2, reverse, (128, 128)))
                for i in range(4):
                    j = i + delta
                    if 0 <= j < 4:
                        th[i * 128 : i * 128 + 128, j * 128 : j * 128 + 128] = high
                        tl[i * 128 : i * 128 + 128, j * 128 : j * 128 + 128] = low

    def start_edge():
        @pl.when(has_after)
        def _():
            edge.start()

        psf_load.wait()

        build((False, mfh, mfl, tfh, tfl))
        zero = jnp.zeros((32, 512), BF16)
        for ref in (fh, fl, rh, rl):
            ref[0:32, :] = zero
            ref[1504:1536, :] = zero

            @pl.when(b == 0)
            def _():
                for t in range(1, 8):
                    ref[t * 32 : t * 32 + 32, :] = zero

            @pl.when(b == 15)
            def _():
                for t in range(40, 47):
                    ref[t * 32 : t * 32 + 32, :] = zero

    exchange(sbox, rbox, a1s, a1r, start_edge)

    take_messages(rbox, piece)
    group = lax.broadcasted_iota(jnp.int32, (8, 128), 1) >> 5
    for c in range(4):
        seen = rbox[4 * c, 2]
        for q in range(1, 4):
            seen = jnp.where(group == q, rbox[4 * c + q, 2], seen)
        visrow[:, 128 * c : 128 * c + 128] = seen

    def gather(own, everything, send, recv, on_half, on_passed):
        used = []

        def place(h):
            return (h + core) % 2

        def rows(h):
            return pl.ds(pl.multiple_of(128 * place(h), 128), 128)

        def push(w, h, target, source=None):
            copy = pltpu.make_async_remote_copy(
                (everything.at[w] if source is None else source).at[rows(h)], everything.at[w, rows(h)],
                send.at[len(used)], recv.at[w, place(h)], device_id=(target, b), device_id_type=MESH,
            )
            copy.start()
            used.append(copy)

        def landed(w, h):
            pltpu.make_async_remote_copy(
                own.at[rows(h)], everything.at[w, rows(h)], send.at[0], recv.at[w, place(h)],
                device_id=(sibling, b), device_id_type=MESH,
            ).wait_recv()

        right, left, across, far = view_at(1, 0), view_at(3, 0), view_at(0, 1), view_at(2, 0)
        for first, second in ((across, right), (right, left), (left, far), (far, across)):
            push(v, 0, first, own)
            push(v, 1, second, own)
        for h in range(2):
            push(v, h, sibling, own)
            on_half(0, own, v, rows(h), place(h))

        @pl.loop(0, 32)
        def _(t):
            tile = pl.ds(pl.multiple_of(t * 8, 8), 8)
            everything.at[v][tile, :] = own[tile, :]

        def relay(dx, dy, h, targets):
            w = view_at(dx, dy)
            landed(w, h)
            for target in targets:
                push(w, h, target)
            push(w, h, sibling)
            on_half(dx + 4 * dy, everything.at[w], w, rows(h), place(h))

        relay(0, 1, 0, (right, left, far))
        relay(3, 0, 1, (across,))
        relay(1, 0, 1, (across,))
        relay(3, 0, 0, ())
        relay(1, 0, 0, ())
        relay(2, 0, 1, (across,))
        relay(2, 0, 0, ())
        relay(0, 1, 1, ())
        for dx in (3, 1, 2):
            for h in range(2):
                relay(dx, 1, h, ())

        for dy in range(2):
            for dx in range(4):
                w = view_at(dx, dy, 1)
                for h in range(2):
                    landed(w, h)
                    on_passed(everything.at[w], w, rows(h), place(h))

        for copy in used:
            copy.wait_send()

    def edge_copy(d, ref, w, slot):
        return pltpu.make_async_remote_copy(
            ref.at[pl.ds(200 * (1 - slot), 56)], tedge.at[w, slot], ts.at[d, slot], tr.at[w, slot],
            device_id=(v, (b + 17 - 2 * slot) % 16), device_id_type=MESH,
        )

    edge_pass = pltpu.make_async_remote_copy(
        eh.at[core], eh.at[core], ef, er.at[1], device_id=(sibling, b), device_id_type=MESH
    )

    halves = []

    def send_edges(d, ref, w, rows, half):
        target = b - 1 + 2 * half

        @pl.when((target >= 0) & (target < 16))
        def _():
            edge_copy(d, ref, w, 1 - half).start()

        halves.append(d)
        if len(halves) == 2:
            build((True, mah, mal, tah, tal))
        if len(halves) == 8:

            @pl.when(has_before)
            def _():
                edge.wait_recv()
                edge_pass.start()

    gather(piece, gathered, g1s, g1r, send_edges, lambda *rest: None)

    def pass_copy(d, w, slot):
        return pltpu.make_async_remote_copy(
            tedge.at[w, slot], tedge.at[w, slot], tf.at[d, slot], tr.at[w, slot],
            device_id=(sibling, b), device_id_type=MESH,
        )

    flat = gathered.reshape(16 * PIECE, 128)

    def put(plane, half, c, value):
        rows = pl.ds(pl.multiple_of(plane * 32 + 16 * half, 16), 16)
        high, low = split(value)
        fh[rows, 128 * c : 128 * c + 128] = high
        fl[rows, 128 * c : 128 * c + 128] = low

    @pl.loop(0, 32)
    def _(x):
        for half in range(2):
            for c in range(4):
                swapped = jnp.concatenate(
                    [flat[pl.ds(t * 8 * PIECE + x * 8 + half * 4 + c, 8, stride=PIECE), :] for t in range(2)], axis=0
                )
                put(x + 8, half, c, jnp.where(turned, swapped, ec[c, x, 16 * half : 16 * half + 16, :]))

    image_load.wait()
    low_halo = pltpu.make_async_remote_copy(
        redge.at[pl.ds(0, 7)], rhalo.at[1], hs.at[0], hr.at[0],
        device_id=(v, (b + 15) % 16), device_id_type=MESH,
    )
    high_halo = pltpu.make_async_remote_copy(
        redge.at[pl.ds(9, 7)], rhalo.at[0], hs.at[1], hr.at[1],
        device_id=(v, (b + 1) % 16), device_id_type=MESH,
    )

    def ahead(g):
        rows = pl.ds(pl.multiple_of(g * 256, 256), 768)
        high, low = split(dot3(mfh[...], mfl[...], fh[rows, :], fl[rows, :]))
        blurred = dot3(high, low, tfh[...], tfl[...])
        ratio = image[pl.ds(8 * g, 8)].reshape(256, 512) / blurred
        high, low = split(ratio)
        inner = pl.ds(pl.multiple_of(g * 256 + 256, 256), 256)
        rh[inner, :] = high
        rl[inner, :] = low
        return ratio

    ahead(1)

    for slot in range(2):
        here = b > 0 if slot == 0 else b < 15
        there = b < 15 if slot == 0 else b > 0

        @pl.when(here)
        def _():
            for d in (0, 4, 3, 1, 2, 7, 5, 6):
                w = view_at(d % 4, d // 4)
                edge_copy(d, piece, w, slot).wait_recv()
                pass_copy(d, w, slot).start()

        @pl.when(there)
        def _():
            for d in range(8):
                edge_copy(d, piece, v, slot).wait_send()

    ahead(2)

    edge_flat = tedge.reshape(16 * 112, 128)

    @pl.when(has_before)
    def _():
        edge_pass.wait_send()

    @pl.when(has_after)
    def _():
        edge.wait_send()

    @pl.when(has_after)
    def _():
        pltpu.make_async_remote_copy(
            eh.at[1 - core], eh.at[1 - core], ef, er.at[1], device_id=(sibling, b), device_id_type=MESH
        ).wait_recv()

    for slot in range(2):
        here = b > 0 if slot == 0 else b < 15

        @pl.when(here)
        def _():
            for d in range(8):
                pass_copy(d, view_at(d % 4, d // 4), slot).wait_send()
                pass_copy(d, view_at(d % 4, d // 4, 1), slot).wait_recv()

            @pl.loop(0, 7)
            def _(x):
                for half in range(2):
                    for c in range(4):
                        start = slot * 56 + x * 8 + half * 4 + c
                        swapped = jnp.concatenate(
                            [edge_flat[pl.ds(t * 896 + start, 8, stride=112), :] for t in range(2)], axis=0
                        )
                        own = eh[slot, x, 16 * half : 16 * half + 16, 128 * c : 128 * c + 128]
                        put(x + 1 + 39 * slot, half, c, jnp.where(turned, swapped, own))

    @pl.loop(0, 2)
    def _(i):
        redge[pl.ds(8 * i, 8)] = ahead(3 * i).reshape(8, 32, 512)

        @pl.when((i == 0) & (b > 0))
        def _():
            low_halo.start()

        @pl.when((i == 1) & (b < 15))
        def _():
            high_halo.start()

    lflat = lp.reshape(16 * PIECE, 128)
    flag = jnp.full((8, 128), jnp.where(turned, 1.0, 0.0), F32)
    for w in range(16):
        lp[w, 0:8, :] = flag

    def back(g, place):
        rows = pl.ds(pl.multiple_of(g * 256, 256), 768)
        high, low = split(dot3(mah[...], mal[...], rh[rows, :], rl[rows, :]))
        correction[...] = dot3(high, low, tah[...], tal[...]).reshape(8, 32, 512)

        @pl.loop(0, 8)
        def _(k):
            seen = jnp.where(visible[0, g * 8 + k] == 1, 1.0, 0.0)
            for c in range(4):
                weight = jnp.where(turned, visrow[:, 128 * c : 128 * c + 128], jnp.full((8, 128), seen, F32))
                for t in range(4):
                    term = weight * jnp.log(correction[k, 8 * t : 8 * t + 8, 128 * c : 128 * c + 128])
                    start = (8 * (t % 2)) * PIECE + (place + k) * 8 + 8 + (t // 2) * 4 + c
                    lflat[pl.ds(start, 8, stride=PIECE), :] = term

    def direct(part, other, origin):
        rows = pl.ds(0, 136) if part == 0 else pl.ds(136, 128)
        return pltpu.make_async_remote_copy(
            lp.at[other, rows], rb.at[origin, rows], rs.at[part, other], rr.at[part, origin],
            device_id=(other, b), device_id_type=MESH,
        )

    def send_part(part):
        for which, order in ((0, [(1, 0, 0), (3, 0, 0), (0, 1, 0), (1, 0, 1), (3, 0, 1), (0, 1, 1), (2, 0, 0), (1, 1, 0), (3, 1, 0), (2, 0, 1), (1, 1, 1), (3, 1, 1), (2, 1, 0), (2, 1, 1), (0, 0, 1)]), (1, [(1, 1, 0), (3, 1, 0), (0, 1, 0), (2, 1, 0), (1, 1, 1), (3, 1, 1), (0, 1, 1), (2, 1, 1), (1, 0, 0), (3, 0, 0), (2, 0, 0), (1, 0, 1), (3, 0, 1), (2, 0, 1), (0, 0, 1)])):
            @pl.when(core == which)
            def _():
                for dx, dy, dc in order:
                    direct_to = view_at(dx, dy, dc)
                    direct(part, direct_to, v).start()

    @pl.loop(0, 2)
    def _(i):
        back(i + 1, 8 * i)

    send_part(0)

    def take_halo(slot):
        @pl.loop(0, 7)
        def _(t):
            high, low = split(rhalo[slot, t])
            rows = pl.ds(pl.multiple_of((t + 1 + 39 * slot) * 32, 32), 32)
            rh[rows, :] = high
            rl[rows, :] = low

    @pl.when(b > 0)
    def _():
        low_halo.wait_send()
        high_halo.wait_recv()
        take_halo(0)

    @pl.when(b < 15)
    def _():
        high_halo.wait_send()
        low_halo.wait_recv()
        take_halo(1)

    @pl.loop(0, 2)
    def _(i):
        back(3 * i, 16 + 8 * i)

    send_part(1)

    def sums(z, place):
        rows = pl.ds(pl.multiple_of(place * 8 + 8, 8), 8)
        up = jnp.zeros((8, 128), F32)
        tp = jnp.zeros((8, 128), F32)
        for w in range(16):
            term = rb[w, rows, :]
            share = term * rb[w, 0:8, :]
            tp = tp + share
            up = up + (term - share)
        rows = pl.ds(pl.multiple_of(z * 8, 8), 8)
        upiece[rows, :] = up
        tpiece[rows, :] = tp

    def take_part(part):
        @pl.loop(0, 17 - part)
        def _(t):
            rows = pl.ds(pl.multiple_of(t * 8 + 136 * part, 8), 8)
            rb.at[v][rows, :] = lp.at[v][rows, :]

        @pl.loop(1, 16)
        def _(d):
            other = (v + d) % 16
            direct(part, other, other).wait_recv()

    take_part(0)

    @pl.loop(0, 16)
    def _(t):
        sums(t + 8, t)

    take_part(1)

    @pl.loop(0, 16)
    def _(t):
        sums(t + 16 * (t // 8), t + 16)

    for part in range(2):
        @pl.loop(1, 16)
        def _(d):
            other = (v + d) % 16
            direct(part, other, other).wait_send()

    make_messages(lambda half, c: tpiece[pl.ds(half * 4 + c, 32, stride=8), :], sbox2)
    exchange(sbox2, rbox2, a2s, a2r)
    take_messages(rbox2, ttpiece)
    upiece[...] = epiece[...] * jnp.exp((upiece[...] + ttpiece[...]) * (1.0 / 16.0))

    def out_copy(ref, w, rows, half):
        return pltpu.make_async_copy(ref.at[rows], o_hbm.at[w, rows], os.at[w, half])

    gather(
        upiece, gathered2, g2s, g2r,
        lambda d, ref, w, rows, half: out_copy(ref, w, rows, half).start(),
        lambda ref, w, rows, half: out_copy(ref, w, rows, half).start(),
    )

    @pl.loop(0, 16)
    def _(w):
        for half in range(2):
            out_copy(upiece, w, pl.ds(128 * half, 128), half).wait()


def reorder(p_hbm, o_hbm, pieces, out, sem_in, sem_out):
    loads, stores = [], []
    for i in range(4):
        part = pl.ds(64 * i, 64)
        loads.append(pltpu.make_async_copy(p_hbm.at[:, part], pieces.at[:, part, :], sem_in.at[i]))
        stores.append(pltpu.make_async_copy(out.at[pl.ds(8 * i, 8)], o_hbm.at[pl.ds(8 * i, 8)], sem_out.at[i]))
    for load in loads:
        load.start()
    flat = pieces.reshape(16 * PIECE, 128)
    for i in range(4):
        loads[i].wait()

        @pl.loop(8 * i, 8 * i + 8)
        def _(z):
            for t in range(4):
                for c in range(4):
                    start = (8 * (t % 2)) * PIECE + z * 8 + (t // 2) * 4 + c
                    out[z, 8 * t : 8 * t + 8, 128 * c : 128 * c + 128] = flat[pl.ds(start, 8, stride=PIECE), :]

        stores[i].start()
    for store in stores:
        store.wait()


def shards(estimate, image, psf, perm, shift, visible):
    smem = pl.BlockSpec(memory_space=pltpu.SMEM)
    hbm = pl.BlockSpec(memory_space=pl.ANY)
    vmem = pltpu.VMEM
    dma = pltpu.SemaphoreType.DMA
    pieces = pl.pallas_call(
        kernel,
        out_shape=jax.ShapeDtypeStruct((16, 256, 128), F32),
        in_specs=[hbm] + [smem] * 3 + [hbm] * 2,
        out_specs=hbm,
        scratch_shapes=[
            pltpu.SMEM((3, 1, 15), F32),
            vmem((4, 32, 32, 128), F32),
            vmem((32, 32, 512), F32),
            vmem((2, 7, 32, 512), F32),
            vmem((16, 2, 56, 128), F32),
        ]
        + [vmem((1536, 512), BF16)] * 4
        + [vmem((16, 32, 512), F32), vmem((2, 7, 32, 512), F32)]
        + [vmem((256, 768), BF16)] * 4
        + [vmem((512, 512), BF16)] * 4
        + [
            vmem((16, 3, 8, 128), F32),
            vmem((16, 3, 8, 128), F32),
            vmem((16, 2, 8, 128), F32),
            vmem((16, 2, 8, 128), F32),
            vmem((8, 512), F32),
            vmem((256, 128), F32),
            vmem((256, 128), F32),
            vmem((16, PIECE, 128), F32),
            vmem((8, 32, 512), F32),
            vmem((16, PIECE, 128), F32),
            vmem((16, PIECE, 128), F32),
            vmem((256, 128), F32),
            vmem((256, 128), F32),
            vmem((256, 128), F32),
            vmem((16, 256, 128), F32),
            dma((6,)),
            dma((16, 2)),
        ]
        + [dma((16,))] * 4
        + [dma((30,)), dma((16, 2))] * 2
        + [dma, dma((2,)), dma]
        + [dma((8, 2)), dma((16, 2)), dma((8, 2))]
        + [dma((2,)), dma((2,)), dma((2, 16)), dma((2, 16))],
        compiler_params=pltpu.CompilerParams(
            collective_id=0, has_side_effects=True, vmem_limit_bytes=60 * 1024 * 1024
        ),
    )(jnp.transpose(psf, (1, 0, 2)), perm, shift, visible, estimate, image)
    return pl.pallas_call(
        reorder,
        out_shape=jax.ShapeDtypeStruct(estimate.shape, F32),
        in_specs=[hbm],
        out_specs=hbm,
        scratch_shapes=[vmem((16, PIECE, 128), F32), vmem((32, 32, 512), F32), dma((4,)), dma((4,))],
    )(pieces)


def solution(mesh):
    placed = (
        P("bulk", None, None),
        P("view", "bulk", None, None),
        P("view", None, None),
        P("view"),
        P("view"),
        P("view", "bulk"),
    )
    return jax.shard_map(
        shards, mesh=mesh, in_specs=placed, out_specs=P("bulk", None, None), check_vma=False
    )
```
